256 devices in a mesh: seq: 64 (over z_lo, y, x, core), head: 4 (over z_hi).
Axes of the slice: x: 4, y: 4, z: 8 (z_hi: 4, z_lo: 2; z = z_hi * 2 + z_lo), core: 2. Of those that a mesh axis runs over, the one named last changes fastest.
Arguments:
- queries: bfloat16 [8192, 6144], P('seq', 'head'), may hold values from -60 to 60
- keys: bfloat16 [8192, 6144], P('seq', 'head'), may hold values from -6 to 6
- values: bfloat16 [8192, 6144], P('seq', 'head'), may hold values from -6 to 6
- band: int32 [48], P('head'), may hold values from 16 to 64
- picks: int32 [64, 16], P('seq'), may hold values from 0 to 127, as said below
- w_out: bfloat16 [6144, 6144], P('seq', 'head'), may hold values from -0.078125 to 0.078125
Outputs:
- output: bfloat16 [8192, 6144], P(('seq', 'head'))
The draws below stay inside these ranges and needn't reach their ends.
Inputs may be any that keep to these rules, and one draw needn't show every extreme that they name: The 16 entries of a row of picks are distinct.
All inputs are finite; a program needn't handle non-finite values.
Results may differ from the reference program's by a relative error of at most 0.015.
Values may be sent and summed in bfloat16 or wider, within the bound.
A program may use at most 128 MiB of HBM per device.

```python
import math
import jax
import jax.numpy as jnp
from jax import lax

HEADS = 48
HD = 128
DW = 6144
BLOCK = 128
SUMS = 16
TOKENS = 8192
NBLOCKS = 64
FEAT = 6144


def key_field(key):
    base = jax.random.fold_in(key, 7)
    field = jnp.clip(jax.random.normal(base, (TOKENS, FEAT), jnp.float32), -6.0, 6.0)
    return field


def draw_queries(key, part):
    other = jax.random.fold_in(key, 8)
    return (3.0 * jnp.clip(jax.random.normal(other, (TOKENS, FEAT), jnp.float32), -6.0, 6.0)).astype(jnp.bfloat16)


def draw_keys(key, part):
    field = key_field(key)
    return field.astype(jnp.bfloat16)


def draw_band(key, part):
    lowest = max(2, BLOCK // 8)
    highest = BLOCK // 2
    widths = jax.random.randint(jax.random.fold_in(key, 3), (HEADS,), lowest, highest + 1)
    order = jax.random.permutation(jax.random.fold_in(key, 4), HEADS)
    widths = widths.at[order[0]].set(highest)
    widths = widths.at[order[1]].set(lowest)
    return widths.astype(jnp.int32)


def draw_picks(key, part):
    raw = jax.random.randint(jax.random.fold_in(key, 5), (NBLOCKS, BLOCK), 0, 1 << 20)
    scores = raw * BLOCK + jnp.arange(BLOCK, dtype=jnp.int32)[None, :]
    unused, chosen = lax.top_k(scores, SUMS)
    return chosen.astype(jnp.int32)


def levels(rng, shape, shards, least, high):
    level, own = 1.0, jax.random.fold_in(rng, 6)
    for dim, parts in shards:
        steps = jnp.exp(jax.random.uniform(jax.random.fold_in(own, dim), (parts,), jnp.float32, least / len(shards), high / len(shards)))
        level = level * jnp.repeat(steps, shape[dim] // parts).reshape([-1 if axis == dim else 1 for axis in range(len(shape))])
    return level


def bell_draw(own_key, shape, scale, limit, shards=(), held_as=jnp.bfloat16):
    loudness = levels(own_key, shape, shards, -0.22, 0.18) if shards else 1.0
    entries = jax.random.normal(own_key, shape, jnp.float32) * scale * loudness
    return jnp.minimum(jnp.maximum(entries, -limit), limit).astype(held_as)


def setup_inputs(seed: int = 0) -> dict:
    key_of = jax.random.split(jax.random.key(seed), 7)
    return {
        "queries": draw_queries(jax.random.fold_in(key_of[6], 71), 0),
        "keys": draw_keys(jax.random.fold_in(key_of[6], 71), 0),
        "values": bell_draw(key_of[2], (TOKENS, FEAT), 1.0, 6.0, ((0, 64), (1, 4))),
        "band": draw_band(jax.random.fold_in(key_of[6], 71), 0),
        "picks": draw_picks(jax.random.fold_in(key_of[6], 71), 0),
        "w_out": bell_draw(key_of[5], (DW, FEAT), FEAT ** -0.5, 0.078125, ((0, 64), (1, 4))),
    }


NEGATIVE_FILL = -1e+30

def reference(queries, keys, values, band, picks, w_out):
    count = TOKENS // BLOCK
    shape_four = (count, BLOCK, HEADS, HD)
    query_blocks = queries.reshape(shape_four)
    key_blocks = keys.reshape(shape_four)
    value_blocks = values.reshape(shape_four)
    chosen = picks[:, :, None, None]
    summary_keys = jnp.take_along_axis(key_blocks, chosen, axis=1).reshape(count * SUMS, HEADS, HD).astype(jnp.float32)
    summary_values = jnp.take_along_axis(value_blocks, chosen, axis=1).reshape(count * SUMS, HEADS, HD).astype(jnp.float32)
    owner = jnp.arange(count * SUMS, dtype=jnp.int32) // SUMS
    zero_block = jnp.zeros((1, BLOCK, HEADS, HD), keys.dtype)
    prior_keys = jnp.concatenate([zero_block, key_blocks[:-1]], 0)
    prior_values = jnp.concatenate([zero_block, value_blocks[:-1]], 0)
    scale = 1.0 / math.sqrt(HD)

    def one_block(item):
        number, query, own_keys, own_values, back_keys, back_values = item
        window_keys = jnp.concatenate([back_keys, own_keys], 0).astype(jnp.float32)
        window_values = jnp.concatenate([back_values, own_values], 0).astype(jnp.float32)
        query_wide = query.astype(jnp.float32)
        near = jnp.einsum('uhd,thd->hut', query_wide, window_keys) * scale
        query_pos = number * BLOCK + jnp.arange(BLOCK, dtype=jnp.int32)
        key_pos = number * BLOCK - BLOCK + jnp.arange(2 * BLOCK, dtype=jnp.int32)
        key_grid = key_pos[None, None, :]
        query_grid = query_pos[None, :, None]
        near_ok = (key_grid <= query_grid) & (key_grid > query_grid - band[:, None, None]) & (key_grid >= 0)
        far = jnp.einsum('uhd,shd->hus', query_wide, summary_keys) * scale
        far_ok = jnp.broadcast_to((owner < number)[None, None, :], far.shape)
        valid = jnp.concatenate([near_ok, far_ok], -1)
        scores = jnp.concatenate([near, far], -1)
        scores = jnp.where(valid, scores, NEGATIVE_FILL)
        largest = lax.optimization_barrier(jnp.max(scores, axis=-1, keepdims=True))
        weights = jnp.where(valid, jnp.exp(scores - largest), 0.0)
        total = lax.optimization_barrier(jnp.sum(weights, axis=-1, keepdims=True))
        rounded = lax.optimization_barrier(weights.astype(jnp.bfloat16)).astype(jnp.float32)
        both_values = jnp.concatenate([window_values, summary_values], 0)
        mixed = jnp.einsum('hut,thd->hud', rounded, both_values) / total
        return mixed.transpose(1, 0, 2).reshape(BLOCK, HEADS * HD).astype(jnp.bfloat16)
    numbers = jnp.arange(count, dtype=jnp.int32)
    attention = lax.map(one_block, (numbers, query_blocks, key_blocks, value_blocks, prior_keys, prior_values))
    attention = attention.reshape(TOKENS, HEADS * HD)
    return jnp.dot(attention, w_out.T, preferred_element_type=jnp.float32).astype(jnp.bfloat16)
```

```python
import functools
import math

import jax
import jax.numpy as jnp
from jax import lax
from jax.experimental import pallas as pl
from jax.experimental.pallas import tpu as pltpu
from jax.sharding import PartitionSpec as P

BLOCK = 128
HALF = 64
HD = 128
SUMS = 16
NX, NY, NZ, NC, NH = 4, 4, 2, 2, 4
NEG = -1e30
MESH = pl.DeviceIdType.MESH
HBM = pl.BlockSpec(memory_space=pltpu.HBM)
VMEM = pl.BlockSpec(memory_space=pltpu.VMEM)


def coords():
    s = lax.axis_index("seq")
    h = lax.axis_index("head")
    return s // 32, (s // 8) % 4, (s // 2) % 4, s % 2, h


def device(z, y, x, c, h):
    return (((z * NY + y) * NX + x) * NC + c, h)


class Copies:
    def __init__(self, send, recv):
        self.send, self.recv, self.used = send, recv, 0
        self.started = []

    def remote(self, src, dst, to):
        n = self.used
        self.used += 1
        copy = pltpu.make_async_remote_copy(
            src_ref=src,
            dst_ref=dst,
            send_sem=self.send.at[n],
            recv_sem=self.recv.at[n],
            device_id=to,
            device_id_type=MESH,
        )
        copy.start()
        self.started.append(copy)
        return copy

    def finish(self):
        for copy in self.started:
            copy.wait_send()


def greet(partners):
    barrier = pltpu.get_barrier_semaphore()
    for partner in partners:
        pl.semaphore_signal(barrier, inc=1, device_id=partner, device_id_type=MESH)
    pl.semaphore_wait(barrier, len(partners))


GATHER_COPIES = 80


def gather_kernel(
    ks_ref, vs_ref, tk_ref, tv_ref, w_ref,
    kg_ref, vg_ref, pk_ref, pv_ref, wg_ref,
    send, recv, local,
):
    z, y, x, c, h = coords()
    s = lax.axis_index("seq")
    at = lambda dz=0, dy=0, dx=0, dc=0: device(
        (z + dz) % NZ, (y + dy) % NY, (x + dx) % NX, (c + dc) % NC, h
    )
    zl, core = at(dz=1), at(dc=1)
    xr, xl, yr, yl = at(dx=1), at(dx=3), at(dy=1), at(dy=3)
    after, before = ((s + 1) % 64, h), ((s + 63) % 64, h)
    greet([zl, core, xr, xl, yr, yl, after, before])
    copies = Copies(send, recv)
    lo, hi = pl.ds(0, SUMS), pl.ds(SUMS, SUMS)
    zs = pl.ds(z * SUMS, SUMS)
    pairs = ((ks_ref, kg_ref), (vs_ref, vg_ref))

    zcopies, owns = [], []
    for i, (own, full) in enumerate(pairs):
        copy = pltpu.make_async_copy(own, full.at[c, y, x, zs], local.at[i])
        copy.start()
        owns.append(copy)
        zcopies.append(copies.remote(own, full.at[c, y, x, zs], zl))
    wown = pltpu.make_async_copy(w_ref, wg_ref.at[y, z], local.at[2])
    wown.start()
    tails = [
        copies.remote(tk_ref, pk_ref, after),
        copies.remote(tv_ref, pv_ref, after),
    ]
    wz = copies.remote(w_ref, wg_ref.at[y, z], zl)
    for copy in owns:
        copy.wait()
    for copy in zcopies:
        copy.wait_recv()

    ym, yp, yo = (y + 3) % NY, (y + 1) % NY, (y + 2) % NY
    xm, xp, xo = (x + 3) % NX, (x + 1) % NX, (x + 2) % NX
    first = []
    for own, full in pairs:
        here = full.at[c, y, x]
        first.append((copies.remote(here, here, yr), copies.remote(here, here, yl)))
    along = {}

    def spread(i, row):
        full = pairs[i][1]
        here = full.at[c, row, x]
        along[i, len([k for k in along if k[0] == i])] = (
            copies.remote(here, here, xr),
            copies.remote(here, here, xl),
        )

    for i in range(2):
        spread(i, y)
    second = []
    for i, (own, full) in enumerate(pairs):
        up, down = first[i]
        up.wait_recv()
        piece = full.at[c, ym, x, lo]
        a = copies.remote(piece, piece, yr)
        spread(i, ym)
        down.wait_recv()
        piece = full.at[c, yp, x, hi]
        b = copies.remote(piece, piece, yl)
        spread(i, yp)
        second.append((a, b))
    wown.wait()
    wz.wait_recv()
    here = wg_ref.at[y]
    wup, wdown = copies.remote(here, here, yr), copies.remote(here, here, yl)
    for i in range(2):
        for copy in second[i]:
            copy.wait_recv()
        spread(i, yo)
    across = []
    for i, (own, full) in enumerate(pairs):
        here = full.at[c, :, x]
        across.append(copies.remote(here, here, core))
    opposite = []
    rows = (y, ym, yp, yo)
    for n in range(4):
        for i, (own, full) in enumerate(pairs):
            right, left = along[i, n]
            right.wait_recv()
            piece = full.at[c, rows[n], xm, lo]
            a = copies.remote(piece, piece, xr)
            left.wait_recv()
            piece = full.at[c, rows[n], xp, hi]
            b = copies.remote(piece, piece, xl)
            opposite.append((a, b))
    wup.wait_recv()
    piece = wg_ref.at[ym, 0]
    wa = copies.remote(piece, piece, yr)
    wdown.wait_recv()
    piece = wg_ref.at[yp, 1]
    wb = copies.remote(piece, piece, yl)
    for i, (own, full) in enumerate(pairs):
        for col in (xm, xp):
            here = full.at[c, :, col]
            across.append(copies.remote(here, here, core))
    for a, b in opposite:
        a.wait_recv()
        b.wait_recv()
    for i, (own, full) in enumerate(pairs):
        here = full.at[c, :, xo]
        across.append(copies.remote(here, here, core))
    for copy in across + tails + [wa, wb]:
        copy.wait_recv()
    copies.finish()


def gather(ks, vs, tk, tv, w):
    feat = ks.shape[1]
    full = jax.ShapeDtypeStruct((NC, NY, NX, NZ * SUMS, feat), ks.dtype)
    tail = jax.ShapeDtypeStruct(tk.shape, tk.dtype)
    return pl.pallas_call(
        gather_kernel,
        out_shape=(
            full, full, tail, tail,
            jax.ShapeDtypeStruct((NY, NZ) + w.shape, w.dtype),
        ),
        in_specs=[HBM] * 5,
        out_specs=(HBM,) * 5,
        scratch_shapes=[
            pltpu.SemaphoreType.DMA((GATHER_COPIES,)),
            pltpu.SemaphoreType.DMA((GATHER_COPIES,)),
            pltpu.SemaphoreType.DMA((3,)),
        ],
        compiler_params=pltpu.CompilerParams(collective_id=0, has_side_effects=True),
        name="gather",
    )(ks, vs, tk, tv, w)


HEADS_PER_STEP = 2


def attend_kernel(
    place_ref, band_ref, q_ref, k_ref, v_ref, pk_ref, pv_ref, kg_ref, vg_ref, o_ref
):
    place = place_ref[0]
    factor = math.log2(math.e) / math.sqrt(HD)
    far_keys = NC * NY * NX * NZ * SUMS
    slot = lax.broadcasted_iota(jnp.int32, (1, far_keys), 1)
    owner = (
        ((slot >> 4) & 1) * 32 + ((slot >> 7) & 3) * 8 + ((slot >> 5) & 3) * 2 + (slot >> 9)
    )
    far_bias = jnp.where(owner < place, 0.0, NEG)
    row = lax.broadcasted_iota(jnp.int32, (BLOCK, BLOCK + HALF), 0)
    col = lax.broadcasted_iota(jnp.int32, (BLOCK, BLOCK + HALF), 1)
    back = row + HALF - col
    causal = (back >= 0) & ((col >= HALF) | (place > 0))
    nt = (((1,), (1,)), ((), ()))
    for i in range(HEADS_PER_STEP):
        band = band_ref[pl.program_id(0) * HEADS_PER_STEP + i]
        cols = pl.ds(i * HD, HD)
        q = q_ref[:, cols]
        near_k = jnp.concatenate([pk_ref[:, cols], k_ref[:, cols]], 0)
        near_v = jnp.concatenate([pv_ref[:, cols], v_ref[:, cols]], 0)
        near = lax.dot_general(q, near_k, nt, preferred_element_type=jnp.float32)
        far = lax.dot_general(q, kg_ref[:, cols], nt, preferred_element_type=jnp.float32)
        near = jnp.where(causal & (back < band), near, NEG)
        far = far + far_bias
        top = jnp.maximum(
            jnp.max(near, axis=1, keepdims=True), jnp.max(far, axis=1, keepdims=True)
        )
        near_w = jnp.exp2((near - top) * factor)
        far_w = jnp.exp2((far - top) * factor)
        total = jnp.sum(near_w, axis=1, keepdims=True) + jnp.sum(far_w, axis=1, keepdims=True)
        mixed = jnp.dot(
            near_w.astype(jnp.bfloat16), near_v, preferred_element_type=jnp.float32
        ) + jnp.dot(
            far_w.astype(jnp.bfloat16), vg_ref[:, cols], preferred_element_type=jnp.float32
        )
        o_ref[:, cols] = (mixed / total).astype(jnp.bfloat16)


def attend(place, band, q, k, v, pk, pv, kg, vg):
    rows, feat = q.shape
    wide = HEADS_PER_STEP * HD
    block = lambda n: pl.BlockSpec((n, wide), lambda i: (0, i))
    smem = pl.BlockSpec(memory_space=pltpu.SMEM)
    far_keys = kg.shape[0]
    return pl.pallas_call(
        attend_kernel,
        out_shape=jax.ShapeDtypeStruct((rows, feat), q.dtype),
        grid=(feat // wide,),
        in_specs=[
            smem, smem, block(rows), block(rows), block(rows),
            block(HALF), block(HALF), block(far_keys), block(far_keys),
        ],
        out_specs=block(rows),
        compiler_params=pltpu.CompilerParams(vmem_limit_bytes=48 << 20),
        name="attend",
    )(place, band, q, k, v, pk, pv, kg, vg)


PROJECT_COPIES = 64
GROUP = NX * NC


def project_kernel(a_ref, w_ref, o_ref, rows, part, early, late, done, send, recv, local):
    z, y, x, c, h = coords()
    at = lambda dx=0, dc=0, dh=0: device(
        z, y, (x + dx) % NX, (c + dc) % NC, (h + dh) % NH
    )
    steps = ((0, 0), (0, 1), (3, 0), (1, 0), (3, 1), (1, 1), (2, 0), (2, 1))
    up, down = at(dh=1), at(dh=3)
    greet([at(dx, dc) for dx, dc in steps[1:]] + [up, down])
    copies = Copies(send, recv)
    sib, xr, xl = at(dc=1), at(dx=1), at(dx=3)
    to_sib = copies.remote(a_ref, rows.at[0], sib)
    to_right = copies.remote(a_ref, rows.at[1], xr)
    to_left = copies.remote(a_ref, rows.at[2], xl)
    arrive = {1: [to_sib], 2: [to_right], 3: [to_left]}
    half_rows = BLOCK // 2
    lo, hi = pl.ds(0, half_rows), pl.ds(half_rows, half_rows)

    def forward(n):
        if n == 2:
            arrive[4] = [copies.remote(rows.at[1], rows.at[3], sib)]
            arrive[6] = [copies.remote(rows.at[1, lo], rows.at[5, lo], xr)]
        if n == 3:
            arrive[5] = [copies.remote(rows.at[2], rows.at[4], sib)]
            arrive[6].append(copies.remote(rows.at[2, hi], rows.at[5, hi], xl))
        if n == 6:
            arrive[7] = [copies.remote(rows.at[5], rows.at[6], sib)]

    quarter = BLOCK // NH
    bit = quarter // 2
    hp, hm, ho = (h + 1) % NH, (h + 3) % NH, (h + 2) % NH
    first, second, last = {}, {}, []

    def product(n):
        if n > 0:
            for copy in arrive[n]:
                copy.wait_recv()
            forward(n)
        block = a_ref[...] if n == 0 else rows[n - 1]
        got = lax.dot_general(
            block, w_ref[...], (((1,), (1,)), ((), ())), preferred_element_type=jnp.float32
        )
        part[n] = got.astype(jnp.bfloat16).reshape(NH, quarter, got.shape[1])
        first[n] = (
            copies.remote(part.at[n, ho, pl.ds(0, bit)], early.at[n, 0], up),
            copies.remote(part.at[n, ho, pl.ds(bit, bit)], early.at[n, 1], down),
        )

    def middle(n):
        a, b = first[n]
        a.wait_recv()
        part[n, hp, pl.ds(0, bit)] = (
            part[n, hp, pl.ds(0, bit)].astype(jnp.float32) + early[n, 0].astype(jnp.float32)
        ).astype(jnp.bfloat16)
        u = copies.remote(part.at[n, hp], late.at[n, 0], up)
        b.wait_recv()
        part[n, hm, pl.ds(bit, bit)] = (
            part[n, hm, pl.ds(bit, bit)].astype(jnp.float32) + early[n, 1].astype(jnp.float32)
        ).astype(jnp.bfloat16)
        second[n] = (u, copies.remote(part.at[n, hm], late.at[n, 1], down))

    def end(n):
        for copy in second[n]:
            copy.wait_recv()
        done[n] = (
            part[n, h].astype(jnp.float32)
            + late[n, 0].astype(jnp.float32)
            + late[n, 1].astype(jnp.float32)
        ).astype(jnp.bfloat16)
        mine = o_ref.at[x * NC + c]
        if n == 0:
            copy = pltpu.make_async_copy(done.at[0], mine, local.at[0])
            copy.start()
            last.append(copy)
        else:
            last.append(copies.remote(done.at[n], mine, at(*steps[n])))

    product(0)
    product(1)
    middle(0)
    product(2)
    middle(1)
    product(3)
    end(0)
    middle(2)
    product(4)
    end(1)
    middle(3)
    product(5)
    end(2)
    middle(4)
    product(6)
    end(3)
    middle(5)
    product(7)
    end(4)
    middle(6)
    end(5)
    middle(7)
    end(6)
    end(7)
    last[0].wait()
    for copy in last[1:]:
        copy.wait_recv()
    copies.finish()


def project(att, w):
    rows, feat = att.shape
    wide = w.shape[0]
    dt = att.dtype
    quarter = rows // NH
    return pl.pallas_call(
        project_kernel,
        out_shape=jax.ShapeDtypeStruct((GROUP, quarter, wide), dt),
        in_specs=[VMEM, VMEM],
        out_specs=VMEM,
        scratch_shapes=[
            pltpu.VMEM((GROUP - 1, rows, feat), dt),
            pltpu.VMEM((GROUP, NH, quarter, wide), dt),
            pltpu.VMEM((GROUP, 2, quarter // 2, wide), dt),
            pltpu.VMEM((GROUP, 2, quarter, wide), dt),
            pltpu.VMEM((GROUP, quarter, wide), dt),
            pltpu.SemaphoreType.DMA((PROJECT_COPIES,)),
            pltpu.SemaphoreType.DMA((PROJECT_COPIES,)),
            pltpu.SemaphoreType.DMA((1,)),
        ],
        compiler_params=pltpu.CompilerParams(
            collective_id=1, has_side_effects=True, vmem_limit_bytes=48 << 20
        ),
        name="project",
    )(att, w)


def local(queries, keys, values, band, picks, w_out):
    place = lax.axis_index("seq")
    tok = queries.shape[0]
    chosen = (picks[0][:, None] == jnp.arange(tok, dtype=jnp.int32)[None, :]).astype(keys.dtype)
    pick = lambda t: jnp.dot(chosen, t, preferred_element_type=jnp.float32).astype(t.dtype)
    kg, vg, pk, pv, wg = gather(
        pick(keys), pick(values), keys[tok - HALF:], values[tok - HALF:], w_out
    )
    feat = queries.shape[1]
    attention = attend(
        place.reshape(1), band, queries, keys, values, pk, pv,
        kg.reshape(-1, feat), vg.reshape(-1, feat),
    )
    got = project(attention, wg.reshape(-1, feat))
    wide = w_out.shape[0]
    parts = got.reshape(GROUP, tok // NH, NY, NZ, wide)
    return parts.transpose(1, 3, 2, 0, 4).reshape(tok // NH, -1)


def solution(mesh):
    placed = (
        P("seq", "head"),
        P("seq", "head"),
        P("seq", "head"),
        P("head"),
        P("seq", None),
        P("seq", "head"),
    )
    return jax.shard_map(
        local, mesh=mesh, in_specs=placed, out_specs=P(("seq", "head"), None), check_vma=False
    )
```

```python
import math

import jax
import jax.numpy as jnp
from jax import lax
from jax.experimental import pallas as pl
from jax.experimental.pallas import tpu as pltpu
from jax.sharding import PartitionSpec as P

BLOCK = 128
HALF = 64
HD = 128
SUMS = 16
HEADS = 12
NX, NY, NZ, NC, NH = 4, 4, 2, 2, 4
GROUP = NX * NC
NEG = -1e30
MESH = pl.DeviceIdType.MESH
UNROLL = 3
COPIES = 136


def device(z, y, x, c, h):
    return (((z * NY + y) * NX + x) * NC + c, h)


class Moved:
    def __init__(self, copy, cond):
        self.copy, self.cond = copy, cond

    def _run(self, what):
        if self.cond is None:
            what()
        else:
            pl.when(self.cond)(what)

    def start(self):
        self._run(self.copy.start)

    def arrived(self):
        self._run(self.copy.wait_recv)


class Copies:
    def __init__(self, send, recv):
        self.send, self.recv = send, recv
        self.made = []

    def remote(self, src, dst, to, cond=None, start=True):
        n = len(self.made)
        copy = pltpu.make_async_remote_copy(
            src_ref=src,
            dst_ref=dst,
            send_sem=self.send.at[n],
            recv_sem=self.recv.at[n],
            device_id=to,
            device_id_type=MESH,
        )
        moved = Moved(copy, cond)
        self.made.append(moved)
        if start:
            moved.start()
        return moved


def greet(partners):
    barrier = pltpu.get_barrier_semaphore()
    for partner in partners:
        pl.semaphore_signal(barrier, inc=1, device_id=partner, device_id_type=MESH)
    pl.semaphore_wait(barrier, len(partners))


def kernel(
    band_ref, picks_ref, q_hbm, k_hbm, v_hbm, w_hbm, o_ref,
    qkv, kv, tails, wg, acc, top, tot, att, rows, part, early, late, done,
    send, recv, local,
):
    s = lax.axis_index("seq")
    h = lax.axis_index("head")
    z, y, x, c = s // 32, (s // 8) % NY, (s // 2) % NX, s % 2
    at = lambda dz=0, dy=0, dx=0, dc=0, dh=0: device(
        (z + dz) % NZ, (y + dy) % NY, (x + dx) % NX, (c + dc) % NC, (h + dh) % NH
    )
    zl, core = at(dz=1), at(dc=1)
    xr, xl, yr, yl = at(dx=1), at(dx=3), at(dy=1), at(dy=3)
    up, down = at(dh=1), at(dh=3)
    after, before = ((s + 1) % 64, h), ((s + 63) % 64, h)
    is0, is1 = z == 0, z == 1
    steps = ((0, 0), (0, 1), (3, 0), (1, 0), (3, 1), (1, 1), (2, 0), (2, 1))
    ym, yp, yo = (y + 3) % NY, (y + 1) % NY, (y + 2) % NY
    xm, xp, xo = (x + 3) % NX, (x + 1) % NX, (x + 2) % NX
    copies = Copies(send, recv)

    loads = []
    for n, ref in enumerate((q_hbm, k_hbm, v_hbm)):
        copy = pltpu.make_async_copy(ref, qkv.at[n], local.at[n])
        copy.start()
        loads.append(copy)
    wown = pltpu.make_async_copy(w_hbm, wg.at[y, z], local.at[3])
    wown.start()
    greet([zl, yr, yl, after, before, up, down] + [at(dx=dx, dc=dc) for dx, dc in steps[1:]])

    tail = pl.ds(BLOCK - HALF, HALF)
    behind = [
        copies.remote(k_hbm.at[tail], tails.at[0], after),
        copies.remote(v_hbm.at[tail], tails.at[1], after),
    ]
    loads[1].wait()
    loads[2].wait()
    spot = lax.broadcasted_iota(jnp.int32, (BLOCK, SUMS), 0)
    chosen = (spot == picks_ref[...]).astype(jnp.bfloat16)
    for i in range(2):
        kv[i, x, c, y, z] = lax.dot_general(
            chosen, qkv[1 + i], (((0,), (0,)), ((), ())), preferred_element_type=jnp.float32
        ).astype(jnp.bfloat16)
    mine = kv.at[:, x, c, y, 0]
    zmove = copies.remote(mine, mine, zl, start=False)
    pl.when(is0)(zmove.copy.start)
    wz = copies.remote(w_hbm, wg.at[y, z], zl)

    zparts = ((1, is1), (0, None))
    along = {}

    def spread(row, n, zz, cond):
        here = kv.at[:, x, c, row, zz]
        along[n, zz] = (copies.remote(here, here, xr, cond), copies.remote(here, here, xl, cond))

    first, second = {}, {}
    for zz, cond in zparts:
        if zz == 0:
            pl.when(is1)(zmove.copy.wait_recv)
        here = kv.at[:, x, c, y, zz]
        first[zz] = (copies.remote(here, here, yr, cond), copies.remote(here, here, yl, cond))
        spread(y, 0, zz, cond)

    factor = math.log2(math.e) / math.sqrt(HD)
    nt = (((1,), (1,)), ((), ()))

    def columns(head):
        return pl.ds(pl.multiple_of(head * HD, HD), HD)

    def near_part():
        row = lax.broadcasted_iota(jnp.int32, (BLOCK, BLOCK + HALF), 0)
        col = lax.broadcasted_iota(jnp.int32, (BLOCK, BLOCK + HALF), 1)
        back = row + HALF - col
        causal = (back >= 0) & ((col >= HALF) | (s > 0))

        def body(i, carry):
            for j in range(UNROLL):
                head = i * UNROLL + j
                cols = columns(head)
                near_k = jnp.concatenate([tails[0, :, cols], qkv[1, :, cols]], 0)
                near_v = jnp.concatenate([tails[1, :, cols], qkv[2, :, cols]], 0)
                score = lax.dot_general(
                    qkv[0, :, cols], near_k, nt, preferred_element_type=jnp.float32
                )
                score = jnp.where(causal & (back < band_ref[head]), score, NEG)
                most = jnp.max(score, axis=1, keepdims=True)
                weight = jnp.exp2((score - most) * factor)
                top[head] = most
                tot[head] = jnp.sum(weight, axis=1, keepdims=True)
                acc[:, cols] = jnp.dot(
                    weight.astype(jnp.bfloat16), near_v, preferred_element_type=jnp.float32
                )
            return carry

        lax.fori_loop(0, HEADS // UNROLL, body, 0)

    def far_part(column, planes):
        count = NC * NY * planes * SUMS
        shift = planes - 1
        slot = lax.broadcasted_iota(jnp.int32, (1, count), 1)
        plane = (slot >> 4) & shift
        owner = plane * 32 + ((slot >> (4 + shift)) & 3) * 8 + column * 2 + (slot >> (6 + shift))
        bias = jnp.where(owner < s, 0.0, NEG)

        def body(i, carry):
            for j in range(UNROLL):
                head = i * UNROLL + j
                cols = columns(head)
                far_k = kv[0, column, :, :, 0:planes, :, cols].reshape(count, HD)
                far_v = kv[1, column, :, :, 0:planes, :, cols].reshape(count, HD)
                score = bias + lax.dot_general(
                    qkv[0, :, cols], far_k, nt, preferred_element_type=jnp.float32
                )
                old = top[head]
                most = jnp.maximum(old, jnp.max(score, axis=1, keepdims=True))
                weight = jnp.exp2((score - most) * factor)
                fade = jnp.exp2((old - most) * factor)
                top[head] = most
                tot[head] = tot[head] * fade + jnp.sum(weight, axis=1, keepdims=True)
                acc[:, cols] = acc[:, cols] * fade + jnp.dot(
                    weight.astype(jnp.bfloat16), far_v, preferred_element_type=jnp.float32
                )
            return carry

        lax.fori_loop(0, HEADS // UNROLL, body, 0)

    def far(column):
        pl.when(is0)(lambda: far_part(column, 1))
        pl.when(is1)(lambda: far_part(column, 2))

    loads[0].wait()
    for copy in behind:
        copy.arrived()
    near_part()

    for zz, cond in zparts:
        first[zz][0].arrived()
        piece = kv.at[0, x, c, ym, zz]
        a = copies.remote(piece, piece, yr, cond)
        spread(ym, 1, zz, cond)
        first[zz][1].arrived()
        piece = kv.at[1, x, c, yp, zz]
        b = copies.remote(piece, piece, yl, cond)
        spread(yp, 2, zz, cond)
        second[zz] = (a, b)
    wown.wait()
    wz.arrived()
    here = wg.at[y]
    wup, wdown = copies.remote(here, here, yr), copies.remote(here, here, yl)
    for zz, cond in zparts:
        for copy in second[zz]:
            copy.arrived()
        spread(yo, 3, zz, cond)

    def across(column):
        moved = []
        for zz, cond in zparts:
            here = kv.at[:, column, c, :, zz]
            moved.append(copies.remote(here, here, core, cond))
        return moved

    opposite = []
    order = (y, ym, yp, yo)

    def pass_on(n):
        for zz, cond in zparts:
            right, left = along[n, zz]
            right.arrived()
            piece = kv.at[0, xm, c, order[n], zz]
            opposite.append(copies.remote(piece, piece, xr, cond))
            left.arrived()
            piece = kv.at[1, xp, c, order[n], zz]
            opposite.append(copies.remote(piece, piece, xl, cond))

    given = across(x)
    pass_on(0)
    for copy in given:
        copy.arrived()
    far(x)
    pass_on(1)
    pass_on(2)
    pass_on(3)
    given_m, given_p = across(xm), across(xp)
    for copy in given_m:
        copy.arrived()
    far(xm)
    wup.arrived()
    piece = wg.at[ym, 0]
    wa = copies.remote(piece, piece, yr)
    wdown.arrived()
    piece = wg.at[yp, 1]
    wb = copies.remote(piece, piece, yl)
    for copy in given_p:
        copy.arrived()
    far(xp)
    for copy in opposite:
        copy.arrived()
    for copy in across(xo):
        copy.arrived()
    far(xo)
    for head in range(HEADS):
        cols = pl.ds(head * HD, HD)
        att[:, cols] = (acc[:, cols] / tot[head]).astype(jnp.bfloat16)

    arrive = {
        1: [copies.remote(att, rows.at[0], core)],
        2: [copies.remote(att, rows.at[1], xr)],
        3: [copies.remote(att, rows.at[2], xl)],
    }
    half_rows = BLOCK // 2
    lo, hi = pl.ds(0, half_rows), pl.ds(half_rows, half_rows)

    def forward(n):
        if n == 2:
            arrive[4] = [copies.remote(rows.at[1], rows.at[3], core)]
            arrive[6] = [copies.remote(rows.at[1, lo], rows.at[5, lo], xr)]
        if n == 3:
            arrive[5] = [copies.remote(rows.at[2], rows.at[4], core)]
            arrive[6].append(copies.remote(rows.at[2, hi], rows.at[5, hi], xl))
        if n == 6:
            arrive[7] = [copies.remote(rows.at[5], rows.at[6], core)]

    quarter = BLOCK // NH
    bit = quarter // 2
    hp, hm, ho = (h + 1) % NH, (h + 3) % NH, (h + 2) % NH
    sent, sums, last = {}, {}, []
    wide = wg.shape[0] * wg.shape[1] * wg.shape[2]
    feat = wg.shape[3]

    def product(n):
        if n > 0:
            for copy in arrive[n]:
                copy.arrived()
            forward(n)
        block = att[...] if n == 0 else rows[n - 1]
        got = lax.dot_general(
            block, wg[...].reshape(wide, feat), nt, preferred_element_type=jnp.float32
        )
        part[n] = got.astype(jnp.bfloat16).reshape(NH, quarter, wide)
        sent[n] = (
            copies.remote(part.at[n, ho, pl.ds(0, bit)], early.at[n, 0], up),
            copies.remote(part.at[n, ho, pl.ds(bit, bit)], early.at[n, 1], down),
        )

    def plus(a, b):
        return a.astype(jnp.float32) + b.astype(jnp.float32)

    def middle(n):
        a, b = sent[n]
        a.arrived()
        area = pl.ds(0, bit)
        part[n, hp, area] = plus(part[n, hp, area], early[n, 0]).astype(jnp.bfloat16)
        u = copies.remote(part.at[n, hp], late.at[n, 0], up)
        b.arrived()
        area = pl.ds(bit, bit)
        part[n, hm, area] = plus(part[n, hm, area], early[n, 1]).astype(jnp.bfloat16)
        sums[n] = (u, copies.remote(part.at[n, hm], late.at[n, 1], down))

    def end(n):
        for copy in sums[n]:
            copy.arrived()
        done[n] = (plus(part[n, h], late[n, 0]) + late[n, 1].astype(jnp.float32)).astype(
            jnp.bfloat16
        )
        place = o_ref.at[x * NC + c]
        if n == 0:
            copy = pltpu.make_async_copy(done.at[0], place, local.at[4])
            copy.start()
            last.append(copy)
        else:
            dx, dc = steps[n]
            last.append(copies.remote(done.at[n], place, at(dx=dx, dc=dc)))

    for copy in (wa, wb):
        copy.arrived()
    product(0)
    product(1)
    middle(0)
    product(2)
    middle(1)
    product(3)
    end(0)
    middle(2)
    product(4)
    end(1)
    middle(3)
    product(5)
    end(2)
    middle(4)
    product(6)
    end(3)
    middle(5)
    product(7)
    end(4)
    middle(6)
    end(5)
    middle(7)
    end(6)
    end(7)
    last[0].wait()
    for copy in last[1:]:
        copy.arrived()

    some = [m for m in copies.made if m.cond is not None]
    pl.when(is0)(zmove.copy.wait_send)

    @pl.when(is1)
    def _():
        for moved in some:
            moved.copy.wait_send()

    for moved in copies.made:
        if moved.cond is None and moved is not zmove:
            moved.copy.wait_send()


def layer(band, picks, q, k, v, w):
    rows, feat = q.shape
    dt = q.dtype
    quarter = rows // NH
    wide = NY * NZ * w.shape[0]
    hbm = pl.BlockSpec(memory_space=pltpu.HBM)
    vmem = pl.BlockSpec(memory_space=pltpu.VMEM)
    smem = pl.BlockSpec(memory_space=pltpu.SMEM)
    return pl.pallas_call(
        kernel,
        out_shape=jax.ShapeDtypeStruct((GROUP, quarter, wide), dt),
        in_specs=[smem, vmem, hbm, hbm, hbm, hbm],
        out_specs=vmem,
        scratch_shapes=[
            pltpu.VMEM((3, rows, feat), dt),
            pltpu.VMEM((2, NX, NC, NY, NZ, SUMS, feat), dt),
            pltpu.VMEM((2, HALF, feat), dt),
            pltpu.VMEM((NY, NZ) + w.shape, dt),
            pltpu.VMEM((rows, feat), jnp.float32),
            pltpu.VMEM((HEADS, rows, 1), jnp.float32),
            pltpu.VMEM((HEADS, rows, 1), jnp.float32),
            pltpu.VMEM((rows, feat), dt),
            pltpu.VMEM((GROUP - 1, rows, feat), dt),
            pltpu.VMEM((GROUP, NH, quarter, wide), dt),
            pltpu.VMEM((GROUP, 2, quarter // 2, wide), dt),
            pltpu.VMEM((GROUP, 2, quarter, wide), dt),
            pltpu.VMEM((GROUP, quarter, wide), dt),
            pltpu.SemaphoreType.DMA((COPIES,)),
            pltpu.SemaphoreType.DMA((COPIES,)),
            pltpu.SemaphoreType.DMA((5,)),
        ],
        compiler_params=pltpu.CompilerParams(
            collective_id=0, has_side_effects=True, vmem_limit_bytes=56 << 20
        ),
        name="layer",
    )(band, picks, q, k, v, w)


def local(queries, keys, values, band, picks, w_out):
    got = layer(band, picks, queries, keys, values, w_out)
    quarter = got.shape[1]
    parts = got.reshape(GROUP, quarter, NY, NZ, w_out.shape[0])
    return parts.transpose(1, 3, 2, 0, 4).reshape(quarter, -1)


def solution(mesh):
    placed = (
        P("seq", "head"),
        P("seq", "head"),
        P("seq", "head"),
        P("head"),
        P("seq", None),
        P("seq", "head"),
    )
    return jax.shard_map(
        local, mesh=mesh, in_specs=placed, out_specs=P(("seq", "head"), None), check_vma=False
    )
```

```python
import math

import jax
import jax.numpy as jnp
from jax import lax
from jax.experimental import pallas as pl
from jax.experimental.pallas import tpu as pltpu
from jax.sharding import PartitionSpec as P

BLOCK = 128
HALF = 64
HD = 128
SUMS = 16
HEADS = 12
NX, NY, NZ, NC, NH = 4, 4, 2, 2, 4
GROUP = NX * NC
NEG = -1e30
MESH = pl.DeviceIdType.MESH
UNROLL = 3
COPIES = 192


def device(z, y, x, c, h):
    return (((z * NY + y) * NX + x) * NC + c, h)


class Moved:
    def __init__(self, copy, cond):
        self.copy, self.cond = copy, cond

    def _run(self, what):
        if self.cond is None:
            what()
        else:
            pl.when(self.cond)(what)

    def start(self):
        self._run(self.copy.start)

    def arrived(self):
        self._run(self.copy.wait_recv)


class Copies:
    def __init__(self, send, recv):
        self.send, self.recv = send, recv
        self.made = []

    def remote(self, src, dst, to, cond=None, start=True):
        n = len(self.made)
        copy = pltpu.make_async_remote_copy(
            src_ref=src,
            dst_ref=dst,
            send_sem=self.send.at[n],
            recv_sem=self.recv.at[n],
            device_id=to,
            device_id_type=MESH,
        )
        moved = Moved(copy, cond)
        self.made.append(moved)
        if start:
            moved.start()
        return moved


def greet(partners):
    barrier = pltpu.get_barrier_semaphore()
    for partner in partners:
        pl.semaphore_signal(barrier, inc=1, device_id=partner, device_id_type=MESH)
    return lambda: pl.semaphore_wait(barrier, len(partners))


def kernel(
    band_ref, picks_ref, q_hbm, k_hbm, v_hbm, w_hbm, o_ref,
    qkv, kv, tails, wg, acc, top, tot, att, rows, part, early, late, done, fin,
    send, recv, local,
):
    s = lax.axis_index("seq")
    h = lax.axis_index("head")
    z, y, x, c = s // 32, (s // 8) % NY, (s // 2) % NX, s % 2
    at = lambda dz=0, dy=0, dx=0, dc=0, dh=0: device(
        (z + dz) % NZ, (y + dy) % NY, (x + dx) % NX, (c + dc) % NC, (h + dh) % NH
    )
    zl, core = at(dz=1), at(dc=1)
    xr, xl, yr, yl = at(dx=1), at(dx=3), at(dy=1), at(dy=3)
    up, down = at(dh=1), at(dh=3)
    after, before = ((s + 1) % 64, h), ((s + 63) % 64, h)
    is0, is1 = z == 0, z == 1
    ym, yp, yo = (y + 3) % NY, (y + 1) % NY, (y + 2) % NY
    xm, xp, xo = (x + 3) % NX, (x + 1) % NX, (x + 2) % NX
    copies = Copies(send, recv)

    loads = []
    for n, ref in enumerate((q_hbm, k_hbm, v_hbm)):
        copy = pltpu.make_async_copy(ref, qkv.at[n], local.at[n])
        copy.start()
        loads.append(copy)
    wown = pltpu.make_async_copy(w_hbm, wg.at[y, z], local.at[3])
    wown.start()
    others = [at(dx=dx, dc=dc) for dx in range(NX) for dc in range(NC) if dx or dc]
    greeted = greet([zl, yr, yl, after, before, up, down] + others)

    loads[1].wait()
    loads[2].wait()
    spot = lax.broadcasted_iota(jnp.int32, (BLOCK, SUMS), 0)
    chosen = (spot == picks_ref[...]).astype(jnp.bfloat16)
    for i in range(2):
        kv[i, x, c, y, z] = lax.dot_general(
            chosen, qkv[1 + i], (((0,), (0,)), ((), ())), preferred_element_type=jnp.float32
        ).astype(jnp.bfloat16)
    greeted()
    mine = kv.at[:, x, c, y, 0]
    zmove = copies.remote(mine, mine, zl, start=False)
    pl.when(is0)(zmove.copy.start)
    zparts = ((1, is1), (0, None))
    along = {}

    def spread(row, n, zz, cond):
        keys, vals = kv.at[0, x, c, row, zz], kv.at[1, x, c, row, zz]
        both = is1 if zz else is0
        along[n, zz] = (
            copies.remote(keys, keys, xr, cond),
            copies.remote(vals, vals, xl, cond),
            copies.remote(vals, vals, xr, both),
            copies.remote(keys, keys, xl, both),
        )

    first, second = {}, {}
    for zz, cond in zparts:
        if zz == 0:
            pl.when(is1)(zmove.copy.wait_recv)
        here = kv.at[:, x, c, y, zz]
        first[zz] = (copies.remote(here, here, yr, cond), copies.remote(here, here, yl, cond))
        spread(y, 0, zz, cond)
        if zz == 1:
            tail = pl.ds(BLOCK - HALF, HALF)
            behind = [
                copies.remote(qkv.at[1, tail], tails.at[0], after),
                copies.remote(qkv.at[2, tail], tails.at[1], after),
            ]
    wown.wait()
    here = wg.at[y, z]
    wz = copies.remote(here, here, zl)
    wfirst = (copies.remote(here, here, yr), copies.remote(here, here, yl))

    factor = math.log2(math.e) / math.sqrt(HD)
    nt = (((1,), (1,)), ((), ()))

    def columns(head):
        return pl.ds(pl.multiple_of(head * HD, HD), HD)

    def near_part():
        row = lax.broadcasted_iota(jnp.int32, (BLOCK, BLOCK + HALF), 0)
        col = lax.broadcasted_iota(jnp.int32, (BLOCK, BLOCK + HALF), 1)
        back = row + HALF - col
        causal = (back >= 0) & ((col >= HALF) | (s > 0))

        def body(i, carry):
            for j in range(UNROLL):
                head = i * UNROLL + j
                cols = columns(head)
                near_k = jnp.concatenate([tails[0, :, cols], qkv[1, :, cols]], 0)
                near_v = jnp.concatenate([tails[1, :, cols], qkv[2, :, cols]], 0)
                score = lax.dot_general(
                    qkv[0, :, cols], near_k, nt, preferred_element_type=jnp.float32
                )
                score = jnp.where(causal & (back < band_ref[head]), score, NEG)
                most = jnp.max(score, axis=1, keepdims=True)
                weight = jnp.exp2((score - most) * factor)
                top[head] = most
                tot[head] = jnp.sum(weight, axis=1, keepdims=True)
                acc[:, cols] = jnp.dot(
                    weight.astype(jnp.bfloat16), near_v, preferred_element_type=jnp.float32
                )
            return carry

        lax.fori_loop(0, HEADS // UNROLL, body, 0)

    def far_part(column, planes):
        count = NC * NY * planes * SUMS
        shift = planes - 1
        slot = lax.broadcasted_iota(jnp.int32, (1, count), 1)
        plane = (slot >> 4) & shift
        owner = plane * 32 + ((slot >> (4 + shift)) & 3) * 8 + column * 2 + (slot >> (6 + shift))
        bias = jnp.where(owner < s, 0.0, NEG)

        def body(i, carry):
            for j in range(UNROLL):
                head = i * UNROLL + j
                cols = columns(head)
                far_k = kv[0, column, :, :, 0:planes, :, cols].reshape(count, HD)
                far_v = kv[1, column, :, :, 0:planes, :, cols].reshape(count, HD)
                score = bias + lax.dot_general(
                    qkv[0, :, cols], far_k, nt, preferred_element_type=jnp.float32
                )
                old = top[head]
                most = jnp.maximum(old, jnp.max(score, axis=1, keepdims=True))
                weight = jnp.exp2((score - most) * factor)
                fade = jnp.exp2((old - most) * factor)
                top[head] = most
                tot[head] = tot[head] * fade + jnp.sum(weight, axis=1, keepdims=True)
                acc[:, cols] = acc[:, cols] * fade + jnp.dot(
                    weight.astype(jnp.bfloat16), far_v, preferred_element_type=jnp.float32
                )
            return carry

        lax.fori_loop(0, HEADS // UNROLL, body, 0)

    def far(column):
        pl.when(is0)(lambda: far_part(column, 1))
        pl.when(is1)(lambda: far_part(column, 2))

    loads[0].wait()
    for copy in behind:
        copy.arrived()
    near_part()

    for zz, cond in zparts:
        first[zz][0].arrived()
        piece = kv.at[0, x, c, ym, zz]
        a = copies.remote(piece, piece, yr, cond)
        spread(ym, 1, zz, cond)
        first[zz][1].arrived()
        piece = kv.at[1, x, c, yp, zz]
        b = copies.remote(piece, piece, yl, cond)
        spread(yp, 2, zz, cond)
        second[zz] = (a, b)
    wz.arrived()
    here = wg.at[y, 1 - z]
    wlast = (copies.remote(here, here, yr), copies.remote(here, here, yl))
    for zz, cond in zparts:
        for copy in second[zz]:
            copy.arrived()
        spread(yo, 3, zz, cond)

    def across(column):
        moved = []
        for zz, cond in zparts:
            here = kv.at[:, column, c, :, zz]
            moved.append(copies.remote(here, here, core, cond))
        return moved

    opposite, lifted = [], []
    order = (y, ym, yp, yo)

    def pass_on(n):
        for zz, cond in zparts:
            both = is1 if zz else is0
            for copy in along[n, zz]:
                copy.arrived()
            row = order[n]
            keys, vals = kv.at[0, xm, c, row, zz], kv.at[1, xp, c, row, zz]
            opposite.append(copies.remote(vals, vals, xl, cond))
            if n < 2:
                opposite.append(copies.remote(keys, keys, xr, cond))
            else:
                other = kv.at[0, xp, c, row, zz]
                opposite.append(copies.remote(other, other, xl, both))
                if zz == 0:
                    opposite.append(copies.remote(keys, keys, xr, is1))
            if zz == 0:
                for there in (kv.at[1, xm, c, row, 0], kv.at[0, xp, c, row, 0]):
                    moved = copies.remote(there, there, zl, start=False)
                    pl.when(is0)(moved.copy.start)
                    lifted.append(moved)

    given = across(x)
    pass_on(0)
    wfirst[0].arrived()
    piece = wg.at[ym, z]
    wa = copies.remote(piece, piece, yr)
    wfirst[1].arrived()
    for copy in given:
        copy.arrived()
    far(x)
    pass_on(1)
    pass_on(2)
    piece = wg.at[yp, 1 - z]
    wb = copies.remote(piece, piece, yl, start=False)

    def onward():
        wlast[0].copy.wait_recv()
        wlast[1].copy.wait_recv()
        wb.copy.start()

    pl.when(is1)(onward)
    pass_on(3)

    @pl.when(is1)
    def _():
        for moved in lifted:
            moved.copy.wait_recv()

    given_m, given_p = across(xm), across(xp)
    for copy in given_m:
        copy.arrived()
    far(xm)
    pl.when(is0)(onward)
    for copy in given_p:
        copy.arrived()
    far(xp)
    for copy in opposite:
        copy.arrived()
    for copy in across(xo):
        copy.arrived()
    far(xo)
    for head in range(HEADS):
        cols = pl.ds(head * HD, HD)
        att[:, cols] = (acc[:, cols] / tot[head]).astype(jnp.bfloat16)

    ahead, astern = 1 + 2 * c, 3 - 2 * c
    steps = (
        (0, 0), (0, 1), (astern, 0), (ahead, 1), (ahead, 0), (astern, 1), (2, 0), (2, 1)
    )
    fore, aft = at(dx=ahead), at(dx=astern)
    arrive = {
        1: [copies.remote(att, rows.at[0], core)],
        2: [copies.remote(att, rows.at[1], fore)],
    }
    half_rows = BLOCK // 2
    lo, hi = pl.ds(0, half_rows), pl.ds(half_rows, half_rows)

    def forward(n):
        if n == 2:
            arrive[3] = [copies.remote(rows.at[1], rows.at[2], core)]
            arrive[6] = [copies.remote(rows.at[1, lo], rows.at[5, lo], fore)]
        if n == 4:
            arrive[5] = [copies.remote(rows.at[3], rows.at[4], core)]
            arrive[6].append(copies.remote(rows.at[3, hi], rows.at[5, hi], aft))
        if n == 6:
            arrive[7] = [copies.remote(rows.at[5], rows.at[6], core)]

    quarter = BLOCK // NH
    bit = quarter // 2
    hp, hm, ho = (h + 1) % NH, (h + 3) % NH, (h + 2) % NH
    sent, sums, last = {}, {}, []
    wide = wg.shape[0] * wg.shape[1] * wg.shape[2]
    feat = wg.shape[3]

    def product(n):
        if n > 0:
            for copy in arrive[n]:
                copy.arrived()
            forward(n)
        block = att[...] if n == 0 else rows[n - 1]
        got = lax.dot_general(
            block, wg[...].reshape(wide, feat), nt, preferred_element_type=jnp.float32
        )
        part[n] = got.astype(jnp.bfloat16).reshape(NH, quarter, wide)
        sent[n] = (
            copies.remote(part.at[n, ho, pl.ds(0, bit)], early.at[n, 0], up),
            copies.remote(part.at[n, ho, pl.ds(bit, bit)], early.at[n, 1], down),
        )

    def plus(a, b):
        return a.astype(jnp.float32) + b.astype(jnp.float32)

    def middle(n):
        a, b = sent[n]
        a.arrived()
        area = pl.ds(0, bit)
        part[n, hp, area] = plus(part[n, hp, area], early[n, 0]).astype(jnp.bfloat16)
        u = copies.remote(part.at[n, hp], late.at[n, 0], up)
        b.arrived()
        area = pl.ds(bit, bit)
        part[n, hm, area] = plus(part[n, hm, area], early[n, 1]).astype(jnp.bfloat16)
        sums[n] = (u, copies.remote(part.at[n, hm], late.at[n, 1], down))

    def end(n):
        for copy in sums[n]:
            copy.arrived()
        done[n] = (plus(part[n, h], late[n, 0]) + late[n, 1].astype(jnp.float32)).astype(
            jnp.bfloat16
        )
        place = fin.at[x * NC + c]
        if n == 0:
            copy = pltpu.make_async_copy(done.at[0], place, local.at[4])
            copy.start()
            last.append(copy)
        else:
            dx, dc = steps[n]
            last.append(copies.remote(done.at[n], place, at(dx=dx, dc=dc)))

    wa.arrived()
    wb.arrived()
    product(0)
    product(1)
    middle(0)
    arrive[4] = [copies.remote(att, rows.at[3], aft)]
    product(2)
    middle(1)
    product(3)
    end(0)
    middle(2)
    product(4)
    end(1)
    middle(3)
    product(5)
    end(2)
    middle(4)
    product(6)
    end(3)
    middle(5)
    product(7)
    end(4)
    middle(6)
    end(5)
    middle(7)
    end(6)
    end(7)
    last[0].wait()
    for copy in last[1:]:
        copy.arrived()
    span = w_hbm.shape[0]
    for n in range(NY * NZ):
        zz, yy = n // NY, n % NY
        cut = slice((yy * NZ + zz) * span, (yy * NZ + zz + 1) * span)
        o_ref[:, n * GROUP * span:(n + 1) * GROUP * span] = jnp.concatenate(
            [fin[g, :, cut] for g in range(GROUP)], axis=1
        )

    for cond in (None, is0, is1):
        chosen = [m for m in copies.made if m.cond is cond and m not in lifted + [zmove]]
        if cond is is0:
            chosen += lifted + [zmove]

        def drain(chosen=chosen):
            for moved in chosen:
                moved.copy.wait_send()

        drain() if cond is None else pl.when(cond)(drain)


def layer(band, picks, q, k, v, w):
    rows, feat = q.shape
    dt = q.dtype
    quarter = rows // NH
    wide = NY * NZ * w.shape[0]
    hbm = pl.BlockSpec(memory_space=pltpu.HBM)
    vmem = pl.BlockSpec(memory_space=pltpu.VMEM)
    smem = pl.BlockSpec(memory_space=pltpu.SMEM)
    return pl.pallas_call(
        kernel,
        out_shape=jax.ShapeDtypeStruct((quarter, GROUP * wide), dt),
        in_specs=[smem, vmem, hbm, hbm, hbm, hbm],
        out_specs=vmem,
        scratch_shapes=[
            pltpu.VMEM((3, rows, feat), dt),
            pltpu.VMEM((2, NX, NC, NY, NZ, SUMS, feat), dt),
            pltpu.VMEM((2, HALF, feat), dt),
            pltpu.VMEM((NY, NZ) + w.shape, dt),
            pltpu.VMEM((rows, feat), jnp.float32),
            pltpu.VMEM((HEADS, rows, 1), jnp.float32),
            pltpu.VMEM((HEADS, rows, 1), jnp.float32),
            pltpu.VMEM((rows, feat), dt),
            pltpu.VMEM((GROUP - 1, rows, feat), dt),
            pltpu.VMEM((GROUP, NH, quarter, wide), dt),
            pltpu.VMEM((GROUP, 2, quarter // 2, wide), dt),
            pltpu.VMEM((GROUP, 2, quarter, wide), dt),
            pltpu.VMEM((GROUP, quarter, wide), dt),
            pltpu.VMEM((GROUP, quarter, wide), dt),
            pltpu.SemaphoreType.DMA((COPIES,)),
            pltpu.SemaphoreType.DMA((COPIES,)),
            pltpu.SemaphoreType.DMA((5,)),
        ],
        compiler_params=pltpu.CompilerParams(
            collective_id=0, has_side_effects=True, vmem_limit_bytes=56 << 20
        ),
        name="layer",
    )(band, picks, q, k, v, w)


def local(queries, keys, values, band, picks, w_out):
    return layer(band, picks, queries, keys, values, w_out)


def solution(mesh):
    placed = (
        P("seq", "head"),
        P("seq", "head"),
        P("seq", "head"),
        P("head"),
        P("seq", None),
        P("seq", "head"),
    )
    return jax.shard_map(
        local, mesh=mesh, in_specs=placed, out_specs=P(("seq", "head"), None), check_vma=False
    )
```

```python
import math

import jax
import jax.numpy as jnp
from jax import lax
from jax.experimental import pallas as pl
from jax.experimental.pallas import tpu as pltpu
from jax.sharding import PartitionSpec as P

BLOCK = 128
HALF = 64
HD = 128
SUMS = 16
HEADS = 12
NX, NY, NZ, NC, NH = 4, 4, 2, 2, 4
GROUP = NX * NC
NEG = -1e30
MESH = pl.DeviceIdType.MESH
COPIES = 160


def device(z, y, x, c, h):
    return (((z * NY + y) * NX + x) * NC + c, h)


class Moved:
    def __init__(self, copy, cond):
        self.copy, self.cond = copy, cond

    def _run(self, what):
        if self.cond is None:
            what()
        else:
            pl.when(self.cond)(what)

    def start(self):
        self._run(self.copy.start)

    def arrived(self):
        self._run(self.copy.wait_recv)


class Copies:
    def __init__(self, send, recv):
        self.send, self.recv = send, recv
        self.made = []

    def remote(self, src, dst, to, cond=None, start=True):
        n = len(self.made)
        copy = pltpu.make_async_remote_copy(
            src_ref=src,
            dst_ref=dst,
            send_sem=self.send.at[n],
            recv_sem=self.recv.at[n],
            device_id=to,
            device_id_type=MESH,
        )
        moved = Moved(copy, cond)
        self.made.append(moved)
        if start:
            moved.start()
        return moved


def greet(partners):
    barrier = pltpu.get_barrier_semaphore()
    for partner in partners:
        pl.semaphore_signal(barrier, inc=1, device_id=partner, device_id_type=MESH)
    return lambda: pl.semaphore_wait(barrier, len(partners))


def kernel(
    band_ref, picks_ref, q_hbm, k_hbm, v_hbm, w_hbm, o_ref,
    qkv, kv, tails, wg, acc, top, tot, rows, part, early, late, done, fin,
    send, recv, local,
):
    s = lax.axis_index("seq")
    h = lax.axis_index("head")
    z, y, x, c = s // 32, (s // 8) % NY, (s // 2) % NX, s % 2
    at = lambda dz=0, dy=0, dx=0, dc=0, dh=0: device(
        (z + dz) % NZ, (y + dy) % NY, (x + dx) % NX, (c + dc) % NC, (h + dh) % NH
    )
    zl, core = at(dz=1), at(dc=1)
    xr, xl, yr, yl = at(dx=1), at(dx=3), at(dy=1), at(dy=3)
    up, down = at(dh=1), at(dh=3)
    after, before = ((s + 1) % 64, h), ((s + 63) % 64, h)
    is0, is1 = z == 0, z == 1
    ym, yp, yo = (y + 3) % NY, (y + 1) % NY, (y + 2) % NY
    xm, xp, xo = (x + 3) % NX, (x + 1) % NX, (x + 2) % NX
    copies = Copies(send, recv)

    loads = []
    for n, ref in enumerate((q_hbm, k_hbm, v_hbm)):
        copy = pltpu.make_async_copy(ref, qkv.at[n], local.at[n])
        copy.start()
        loads.append(copy)
    wown = pltpu.make_async_copy(w_hbm, wg.at[0, z], local.at[3])
    wown.start()
    others = [at(dx=dx, dc=dc) for dx in range(NX) for dc in range(NC) if dx or dc]
    greeted = greet([zl, yr, yl, after, before, up, down] + others)

    loads[1].wait()
    loads[2].wait()
    spot = lax.broadcasted_iota(jnp.int32, (BLOCK, SUMS), 0)
    chosen = (spot == picks_ref[...]).astype(jnp.bfloat16)
    for i in range(2):
        kv[i, x, c, y, z] = lax.dot_general(
            chosen, qkv[1 + i], (((0,), (0,)), ((), ())), preferred_element_type=jnp.float32
        ).astype(jnp.bfloat16)
    greeted()
    mine = kv.at[:, x, c, y, 0]
    zmove = copies.remote(mine, mine, zl, start=False)
    pl.when(is0)(zmove.copy.start)
    zparts = ((1, is1), (0, None))
    along = {}

    def spread(row, n, zz, cond):
        keys, vals = kv.at[0, x, c, row, zz], kv.at[1, x, c, row, zz]
        both = is1 if zz else is0
        along[n, zz] = (
            copies.remote(keys, keys, xr, cond),
            copies.remote(vals, vals, xl, cond),
            copies.remote(vals, vals, xr, both),
            copies.remote(keys, keys, xl, both),
        )

    first, second = {}, {}
    for zz, cond in zparts:
        if zz == 0:
            pl.when(is1)(zmove.copy.wait_recv)
        here = kv.at[:, x, c, y, zz]
        first[zz] = (copies.remote(here, here, yr, cond), copies.remote(here, here, yl, cond))
        spread(y, 0, zz, cond)
    wown.wait()
    here = wg.at[0, z]
    wz = copies.remote(here, here, zl)

    factor = math.log2(math.e) / math.sqrt(HD)
    nt = (((1,), (1,)), ((), ()))

    def absorb(head, keys, vals, score, fresh):
        cols = pl.ds(head * HD, HD)
        most = jnp.max(score, axis=0, keepdims=True)
        if not fresh:
            old = top[head]
            most = jnp.maximum(old, most)
        weight = jnp.exp2((score - most) * factor)
        total = jnp.sum(weight, axis=0, keepdims=True)
        mixed = lax.dot_general(
            vals, weight.astype(jnp.bfloat16), (((0,), (0,)), ((), ())),
            preferred_element_type=jnp.float32,
        )
        if not fresh:
            fade = jnp.exp2((old - most) * factor)
            total = total + tot[head] * fade
            mixed = mixed + acc[:, cols] * fade
        top[head], tot[head] = most, total
        acc[:, cols] = mixed

    def near_part():
        key = lax.broadcasted_iota(jnp.int32, (BLOCK + HALF, BLOCK), 0)
        query = lax.broadcasted_iota(jnp.int32, (BLOCK + HALF, BLOCK), 1)
        back = query + HALF - key
        causal = (back >= 0) & ((key >= HALF) | (s > 0))
        for head in range(HEADS):
            cols = pl.ds(head * HD, HD)
            keys = jnp.concatenate([tails[0, :, cols], qkv[1, :, cols]], 0)
            vals = jnp.concatenate([tails[1, :, cols], qkv[2, :, cols]], 0)
            score = lax.dot_general(
                keys, qkv[0, :, cols], nt, preferred_element_type=jnp.float32
            )
            score = jnp.where(causal & (back < band_ref[head]), score, NEG)
            absorb(head, keys, vals, score, True)

    def far_part(places, planes):
        each = NC * NY * planes * SUMS
        count = each * len(places)
        shift = planes - 1
        slot = lax.broadcasted_iota(jnp.int32, (count, HD), 0)
        column = places[0]
        if len(places) == 2:
            column = jnp.where(slot < each, places[0], places[1])
        owner = (
            ((slot >> 4) & shift) * 32 + ((slot >> (4 + shift)) & 3) * 8
            + column * 2 + ((slot >> (6 + shift)) & 1)
        )
        bias = jnp.where(owner < s, 0.0, NEG)
        for head in range(HEADS):
            cols = pl.ds(head * HD, HD)
            keys, vals = (
                jnp.concatenate(
                    [kv[i, p, :, :, 0:planes, :, cols].reshape(each, HD) for p in places], 0
                )
                for i in range(2)
            )
            score = bias + lax.dot_general(
                keys, qkv[0, :, cols], nt, preferred_element_type=jnp.float32
            )
            absorb(head, keys, vals, score, False)

    for zz, cond in zparts:
        first[zz][0].arrived()
        piece = kv.at[0, x, c, ym, zz]
        a = copies.remote(piece, piece, yr, cond)
        spread(ym, 1, zz, cond)
        first[zz][1].arrived()
        piece = kv.at[1, x, c, yp, zz]
        b = copies.remote(piece, piece, yl, cond)
        spread(yp, 2, zz, cond)
        second[zz] = (a, b)
    tail = pl.ds(BLOCK - HALF, HALF)
    behind = [
        copies.remote(qkv.at[1, tail], tails.at[0], after),
        copies.remote(qkv.at[2, tail], tails.at[1], after),
    ]

    def both_ways(zz):
        here = wg.at[0, zz]
        return (copies.remote(here, wg.at[1, zz], yr), copies.remote(here, wg.at[2, zz], yl))

    wfirst = both_ways(z)
    for zz, cond in zparts:
        for copy in second[zz]:
            copy.arrived()
        spread(yo, 3, zz, cond)
    wz.arrived()
    wlast = both_ways(1 - z)
    wa = copies.remote(wg.at[1, z], wg.at[3, z], yr, start=False)
    wb = copies.remote(wg.at[2, 1 - z], wg.at[3, 1 - z], yl, start=False)

    def w_early():
        wfirst[0].copy.wait_recv()
        wa.copy.start()

    def w_late():
        wfirst[1].copy.wait_recv()
        wlast[0].copy.wait_recv()
        wlast[1].copy.wait_recv()
        wb.copy.start()

    def across(column):
        moved = []
        for zz, cond in zparts:
            here = kv.at[:, column, c, :, zz]
            moved.append(copies.remote(here, here, core, cond))
        return moved

    opposite, lifted = [], []
    order = (y, ym, yp, yo)

    def pass_on(n):
        for zz, cond in zparts:
            both = is1 if zz else is0
            for copy in along[n, zz]:
                copy.arrived()
            row = order[n]
            keys, vals = kv.at[0, xm, c, row, zz], kv.at[1, xp, c, row, zz]
            opposite.append(copies.remote(vals, vals, xl, cond))
            if n < 2:
                opposite.append(copies.remote(keys, keys, xr, cond))
            else:
                other = kv.at[0, xp, c, row, zz]
                opposite.append(copies.remote(other, other, xl, both))
                if zz == 0:
                    opposite.append(copies.remote(keys, keys, xr, is1))
            if zz == 0:
                for there in (kv.at[1, xm, c, row, 0], kv.at[0, xp, c, row, 0]):
                    moved = copies.remote(there, there, zl, start=False)
                    pl.when(is0)(moved.copy.start)
                    lifted.append(moved)

    given = across(x)
    pass_on(0)
    loads[0].wait()
    for copy in behind:
        copy.arrived()
    near_part()
    pass_on(1)
    for copy in given:
        copy.arrived()
    pl.when(is1)(lambda: far_part([x], 2))
    pass_on(2)

    @pl.when(is1)
    def _():
        w_early()
        w_late()

    pass_on(3)

    @pl.when(is1)
    def _():
        for moved in lifted:
            moved.copy.wait_recv()

    given_m, given_p = across(xm), across(xp)
    for copy in given_m:
        copy.arrived()

    @pl.when(is0)
    def _():
        far_part([x, xm], 1)
        w_early()

    pl.when(is1)(lambda: far_part([xm], 2))
    for copy in given_p:
        copy.arrived()
    pl.when(is1)(lambda: far_part([xp], 2))
    for copy in opposite:
        copy.arrived()
    given = across(xo)
    pl.when(is0)(w_late)
    for copy in given:
        copy.arrived()
    pl.when(is0)(lambda: far_part([xp, xo], 1))
    pl.when(is1)(lambda: far_part([xo], 2))
    att = rows.at[0]
    for head in range(HEADS):
        cols = pl.ds(head * HD, HD)
        att[:, cols] = (acc[:, cols] / tot[head]).T.astype(jnp.bfloat16)

    ahead, astern = 1 + 2 * c, 3 - 2 * c
    steps = (
        (0, 0), (0, 1), (astern, 0), (ahead, 1), (ahead, 0), (astern, 1), (2, 0), (2, 1)
    )
    fore, aft = at(dx=ahead), at(dx=astern)
    arrive = {
        1: [copies.remote(att, rows.at[1], core)],
        2: [copies.remote(att, rows.at[2], fore)],
    }
    half_rows = BLOCK // 2
    lo, hi = pl.ds(0, half_rows), pl.ds(half_rows, half_rows)

    def forward(n):
        if n == 2:
            arrive[3] = [copies.remote(rows.at[2], rows.at[3], core)]
            arrive[6] = [copies.remote(rows.at[2, lo], rows.at[6, lo], fore)]
        if n == 4:
            arrive[5] = [copies.remote(rows.at[4], rows.at[5], core)]
            arrive[6].append(copies.remote(rows.at[4, hi], rows.at[6, hi], aft))
        if n == 6:
            arrive[7] = [copies.remote(rows.at[6], rows.at[7], core)]

    quarter = BLOCK // NH
    bit = quarter // 2
    hp, hm, ho = (h + 1) % NH, (h + 3) % NH, (h + 2) % NH
    sent, sums, last = {}, {}, []
    span, feat = w_hbm.shape
    wide = NY * NZ * span

    def pair(n):
        for k in (n, n + 1):
            for copy in arrive.get(k, ()):
                copy.arrived()
            forward(k)
        got = lax.dot_general(
            rows[n:n + 2].reshape(2 * BLOCK, feat), wg[...].reshape(wide, feat), nt,
            preferred_element_type=jnp.float32,
        )
        part[n:n + 2] = got.astype(jnp.bfloat16).reshape(2, NH, quarter, wide)
        for k in (n, n + 1):
            sent[k] = (
                copies.remote(part.at[k, ho, pl.ds(0, bit)], early.at[k, 0], up),
                copies.remote(part.at[k, ho, pl.ds(bit, bit)], early.at[k, 1], down),
            )

    def plus(a, b):
        return a.astype(jnp.float32) + b.astype(jnp.float32)

    def middle(n):
        a, b = sent[n]
        a.arrived()
        area = pl.ds(0, bit)
        part[n, hp, area] = plus(part[n, hp, area], early[n, 0]).astype(jnp.bfloat16)
        there = copies.remote(part.at[n, hp], late.at[n, 0], up)
        b.arrived()
        area = pl.ds(bit, bit)
        part[n, hm, area] = plus(part[n, hm, area], early[n, 1]).astype(jnp.bfloat16)
        sums[n] = (there, copies.remote(part.at[n, hm], late.at[n, 1], down))

    def end(n):
        for copy in sums[n]:
            copy.arrived()
        done[n] = (plus(part[n, h], late[n, 0]) + late[n, 1].astype(jnp.float32)).astype(
            jnp.bfloat16
        )
        place = fin.at[x * NC + c]
        if n == 0:
            copy = pltpu.make_async_copy(done.at[0], place, local.at[4])
            copy.start()
            last.append(copy.wait)
        else:
            dx, dc = steps[n]
            last.append(copies.remote(done.at[n], place, at(dx=dx, dc=dc)).arrived)

    wa.arrived()
    wb.arrived()
    pair(0)
    middle(0)
    arrive[4] = [copies.remote(att, rows.at[4], aft)]
    middle(1)
    pair(2)
    end(0)
    middle(2)
    middle(3)
    pair(4)
    end(1)
    end(2)
    middle(4)
    middle(5)
    pair(6)
    end(3)
    end(4)
    middle(6)
    middle(7)
    end(5)
    end(6)
    end(7)
    for wait in last:
        wait()
    for n, shift in enumerate((0, 3, 1, 2)):
        for zz in range(NZ):
            cut = slice((n * NZ + zz) * span, (n * NZ + zz + 1) * span)
            size = GROUP * span
            start = (zz * NY + (y + shift) % NY) * size
            o_ref[:, pl.ds(pl.multiple_of(start, size), size)] = jnp.concatenate(
                [fin[g, :, cut] for g in range(GROUP)], axis=1
            )

    for cond in (None, is0, is1):
        chosen = [m for m in copies.made if m.cond is cond and m not in lifted + [zmove]]
        if cond is is0:
            chosen += lifted + [zmove]

        def drain(chosen=chosen):
            for moved in chosen:
                moved.copy.wait_send()

        drain() if cond is None else pl.when(cond)(drain)


def layer(band, picks, q, k, v, w):
    rows, feat = q.shape
    dt = q.dtype
    quarter = rows // NH
    wide = NY * NZ * w.shape[0]
    hbm = pl.BlockSpec(memory_space=pltpu.HBM)
    vmem = pl.BlockSpec(memory_space=pltpu.VMEM)
    smem = pl.BlockSpec(memory_space=pltpu.SMEM)
    return pl.pallas_call(
        kernel,
        out_shape=jax.ShapeDtypeStruct((quarter, GROUP * wide), dt),
        in_specs=[smem, vmem, hbm, hbm, hbm, hbm],
        out_specs=vmem,
        scratch_shapes=[
            pltpu.VMEM((3, rows, feat), dt),
            pltpu.VMEM((2, NX, NC, NY, NZ, SUMS, feat), dt),
            pltpu.VMEM((2, HALF, feat), dt),
            pltpu.VMEM((NY, NZ) + w.shape, dt),
            pltpu.VMEM((rows, feat), jnp.float32),
            pltpu.VMEM((HEADS, 1, rows), jnp.float32),
            pltpu.VMEM((HEADS, 1, rows), jnp.float32),
            pltpu.VMEM((GROUP, rows, feat), dt),
            pltpu.VMEM((GROUP, NH, quarter, wide), dt),
            pltpu.VMEM((GROUP, 2, quarter // 2, wide), dt),
            pltpu.VMEM((GROUP, 2, quarter, wide), dt),
            pltpu.VMEM((GROUP, quarter, wide), dt),
            pltpu.VMEM((GROUP, quarter, wide), dt),
            pltpu.SemaphoreType.DMA((COPIES,)),
            pltpu.SemaphoreType.DMA((COPIES,)),
            pltpu.SemaphoreType.DMA((5,)),
        ],
        compiler_params=pltpu.CompilerParams(
            collective_id=0, has_side_effects=True, vmem_limit_bytes=56 << 20
        ),
        name="layer",
    )(band, picks, q, k, v, w)


def local(queries, keys, values, band, picks, w_out):
    return layer(band, picks, queries, keys, values, w_out)


def solution(mesh):
    placed = (
        P("seq", "head"),
        P("seq", "head"),
        P("seq", "head"),
        P("head"),
        P("seq", None),
        P("seq", "head"),
    )
    return jax.shard_map(
        local, mesh=mesh, in_specs=placed, out_specs=P(("seq", "head"), None), check_vma=False
    )
```

```python
import math

import jax
import jax.numpy as jnp
from jax import lax
from jax.experimental import pallas as pl
from jax.experimental.pallas import tpu as pltpu
from jax.sharding import PartitionSpec as P

BLOCK = 128
HALF = 64
HD = 128
SUMS = 16
HEADS = 12
NX, NY, NZ, NC, NH = 4, 4, 2, 2, 4
GROUP = NX * NC
NEG = -1e30
MESH = pl.DeviceIdType.MESH
COPIES = 160


def device(z, y, x, c, h):
    return (((z * NY + y) * NX + x) * NC + c, h)


class Moved:
    def __init__(self, copy, cond):
        self.copy, self.cond = copy, cond

    def _run(self, what):
        if self.cond is None:
            what()
        else:
            pl.when(self.cond)(what)

    def start(self):
        self._run(self.copy.start)

    def arrived(self):
        self._run(self.copy.wait_recv)


class Copies:
    def __init__(self, send, recv):
        self.send, self.recv = send, recv
        self.made = []

    def remote(self, src, dst, to, cond=None, start=True):
        n = len(self.made)
        copy = pltpu.make_async_remote_copy(
            src_ref=src,
            dst_ref=dst,
            send_sem=self.send.at[n],
            recv_sem=self.recv.at[n],
            device_id=to,
            device_id_type=MESH,
        )
        moved = Moved(copy, cond)
        self.made.append(moved)
        if start:
            moved.start()
        return moved


def greet(partners):
    barrier = pltpu.get_barrier_semaphore()
    for partner in partners:
        pl.semaphore_signal(barrier, inc=1, device_id=partner, device_id_type=MESH)
    return lambda: pl.semaphore_wait(barrier, len(partners))


def kernel(
    band_ref, picks_ref, q_hbm, k_hbm, v_hbm, w_hbm, o_ref,
    qkv, kv, tails, wg, acc, top, tot, rows, part, early, late, done, fin,
    send, recv, local,
):
    s = lax.axis_index("seq")
    h = lax.axis_index("head")
    z, y, x, c = s // 32, (s // 8) % NY, (s // 2) % NX, s % 2
    at = lambda dz=0, dy=0, dx=0, dc=0, dh=0: device(
        (z + dz) % NZ, (y + dy) % NY, (x + dx) % NX, (c + dc) % NC, (h + dh) % NH
    )
    zl, core = at(dz=1), at(dc=1)
    xr, xl, yr, yl = at(dx=1), at(dx=3), at(dy=1), at(dy=3)
    up, down = at(dh=1), at(dh=3)
    after, before = ((s + 1) % 64, h), ((s + 63) % 64, h)
    is0, is1 = z == 0, z == 1
    ym, yp, yo = (y + 3) % NY, (y + 1) % NY, (y + 2) % NY
    xm, xp, xo = (x + 3) % NX, (x + 1) % NX, (x + 2) % NX
    copies = Copies(send, recv)

    loads = []
    for n, ref in enumerate((q_hbm, k_hbm, v_hbm)):
        copy = pltpu.make_async_copy(ref, qkv.at[n], local.at[n])
        copy.start()
        loads.append(copy)
    wown = pltpu.make_async_copy(w_hbm, wg.at[0, z], local.at[3])
    wown.start()
    others = [at(dx=dx, dc=dc) for dx in range(NX) for dc in range(NC) if dx or dc]
    greeted = greet([zl, yr, yl, after, before, up, down] + others)

    loads[1].wait()
    loads[2].wait()
    spot = lax.broadcasted_iota(jnp.int32, (BLOCK, SUMS), 0)
    chosen = (spot == picks_ref[...]).astype(jnp.bfloat16)
    for i in range(2):
        kv[i, x, c, y, z] = lax.dot_general(
            chosen, qkv[1 + i], (((0,), (0,)), ((), ())), preferred_element_type=jnp.float32
        ).astype(jnp.bfloat16)
    greeted()
    tail = pl.ds(BLOCK - HALF, HALF)
    behind = [
        copies.remote(qkv.at[1, tail], tails.at[0], after),
        copies.remote(qkv.at[2, tail], tails.at[1], after),
    ]
    mine = kv.at[:, x, c, y, 0]
    zmove = copies.remote(mine, mine, zl, start=False)
    pl.when(is0)(zmove.copy.start)
    zparts = ((1, is1), (0, None))
    along = {}

    def spread(row, n, zz, cond):
        keys, vals = kv.at[0, x, c, row, zz], kv.at[1, x, c, row, zz]
        both = is1 if zz else is0
        along[n, zz] = (
            copies.remote(keys, keys, xr, cond),
            copies.remote(vals, vals, xl, cond),
            copies.remote(vals, vals, xr, both),
            copies.remote(keys, keys, xl, both),
        )

    first, second = {}, {}
    for zz, cond in zparts:
        if zz == 0:
            pl.when(is1)(zmove.copy.wait_recv)
        here = kv.at[:, x, c, y, zz]
        first[zz] = (copies.remote(here, here, yr, cond), copies.remote(here, here, yl, cond))
        spread(y, 0, zz, cond)
    wown.wait()
    here = wg.at[0, z]
    wz = copies.remote(here, here, zl)

    factor = math.log2(math.e) / math.sqrt(HD)
    nt = (((1,), (1,)), ((), ()))

    def absorb(head, keys, vals, score, fresh):
        cols = pl.ds(head * HD, HD)
        most = jnp.max(score, axis=0, keepdims=True)
        if not fresh:
            old = top[head]
            most = jnp.maximum(old, most)
        weight = jnp.exp2((score - most) * factor)
        total = jnp.sum(weight, axis=0, keepdims=True)
        mixed = lax.dot_general(
            vals, weight.astype(jnp.bfloat16), (((0,), (0,)), ((), ())),
            preferred_element_type=jnp.float32,
        )
        if not fresh:
            fade = jnp.exp2((old - most) * factor)
            total = total + tot[head] * fade
            mixed = mixed + acc[:, cols] * fade
        top[head], tot[head] = most, total
        acc[:, cols] = mixed

    def near_part():
        key = lax.broadcasted_iota(jnp.int32, (BLOCK + HALF, BLOCK), 0)
        query = lax.broadcasted_iota(jnp.int32, (BLOCK + HALF, BLOCK), 1)
        back = query + HALF - key
        causal = (back >= 0) & ((key >= HALF) | (s > 0))
        for head in range(HEADS):
            cols = pl.ds(head * HD, HD)
            keys = jnp.concatenate([tails[0, :, cols], qkv[1, :, cols]], 0)
            vals = jnp.concatenate([tails[1, :, cols], qkv[2, :, cols]], 0)
            score = lax.dot_general(
                keys, qkv[0, :, cols], nt, preferred_element_type=jnp.float32
            )
            score = jnp.where(causal & (back < band_ref[head]), score, NEG)
            absorb(head, keys, vals, score, True)

    def far_part(places, planes):
        each = NC * NY * planes * SUMS
        count = each * len(places)
        shift = planes - 1
        slot = lax.broadcasted_iota(jnp.int32, (count, HD), 0)
        column = places[0]
        if len(places) == 2:
            column = jnp.where(slot < each, places[0], places[1])
        owner = (
            ((slot >> 4) & shift) * 32 + ((slot >> (4 + shift)) & 3) * 8
            + column * 2 + ((slot >> (6 + shift)) & 1)
        )
        bias = jnp.where(owner < s, 0.0, NEG)
        for head in range(HEADS):
            cols = pl.ds(head * HD, HD)
            keys, vals = (
                jnp.concatenate(
                    [kv[i, p, :, :, 0:planes, :, cols].reshape(each, HD) for p in places], 0
                )
                for i in range(2)
            )
            score = bias + lax.dot_general(
                keys, qkv[0, :, cols], nt, preferred_element_type=jnp.float32
            )
            absorb(head, keys, vals, score, False)

    for zz, cond in zparts:
        first[zz][0].arrived()
        piece = kv.at[0, x, c, ym, zz]
        a = copies.remote(piece, piece, yr, cond)
        spread(ym, 1, zz, cond)
        first[zz][1].arrived()
        piece = kv.at[1, x, c, yp, zz]
        b = copies.remote(piece, piece, yl, cond)
        spread(yp, 2, zz, cond)
        second[zz] = (a, b)

    def both_ways(zz):
        here = wg.at[0, zz]
        return (copies.remote(here, wg.at[1, zz], yr), copies.remote(here, wg.at[2, zz], yl))

    wfirst = both_ways(z)
    for zz, cond in zparts:
        for copy in second[zz]:
            copy.arrived()
        spread(yo, 3, zz, cond)
    wz.arrived()
    wlast = both_ways(1 - z)
    wa = copies.remote(wg.at[1, z], wg.at[3, z], yr, start=False)
    wb = copies.remote(wg.at[2, 1 - z], wg.at[3, 1 - z], yl, start=False)

    def w_early():
        wfirst[0].copy.wait_recv()
        wa.copy.start()

    def w_late():
        wfirst[1].copy.wait_recv()
        wlast[0].copy.wait_recv()
        wlast[1].copy.wait_recv()
        wb.copy.start()

    def across(column):
        moved = []
        for zz, cond in zparts:
            here = kv.at[:, column, c, :, zz]
            moved.append(copies.remote(here, here, core, cond))
        return moved

    opposite, lifted = [], []
    order = (y, ym, yp, yo)

    def pass_on(n):
        for zz, cond in zparts:
            both = is1 if zz else is0
            for copy in along[n, zz]:
                copy.arrived()
            row = order[n]
            keys, vals = kv.at[0, xm, c, row, zz], kv.at[1, xp, c, row, zz]
            opposite.append(copies.remote(vals, vals, xl, cond))
            if n < 2:
                opposite.append(copies.remote(keys, keys, xr, cond))
            else:
                other = kv.at[0, xp, c, row, zz]
                opposite.append(copies.remote(other, other, xl, both))
                if zz == 0:
                    opposite.append(copies.remote(keys, keys, xr, is1))
            if zz == 0:
                for there in (kv.at[1, xm, c, row, 0], kv.at[0, xp, c, row, 0]):
                    moved = copies.remote(there, there, zl, start=False)
                    pl.when(is0)(moved.copy.start)
                    lifted.append(moved)

    given = across(x)
    pass_on(0)
    loads[0].wait()
    for copy in behind:
        copy.arrived()
    near_part()
    pass_on(1)
    for copy in given:
        copy.arrived()
    pl.when(is1)(lambda: far_part([x], 2))
    pass_on(2)

    pl.when(is1)(w_early)
    pass_on(3)

    @pl.when(is1)
    def _():
        for moved in lifted:
            moved.copy.wait_recv()

    given_m, given_p = across(xm), across(xp)
    for copy in given_m:
        copy.arrived()

    @pl.when(is0)
    def _():
        far_part([x, xm], 1)
        w_early()

    @pl.when(is1)
    def _():
        far_part([xm], 2)
        w_late()

    for copy in given_p:
        copy.arrived()
    pl.when(is1)(lambda: far_part([xp], 2))
    for copy in opposite:
        copy.arrived()
    given = across(xo)
    pl.when(is0)(w_late)
    for copy in given:
        copy.arrived()
    pl.when(is0)(lambda: far_part([xp, xo], 1))
    pl.when(is1)(lambda: far_part([xo], 2))
    att = rows.at[0]
    for head in range(HEADS):
        cols = pl.ds(head * HD, HD)
        att[:, cols] = (acc[:, cols] / tot[head]).T.astype(jnp.bfloat16)

    ahead, astern = 1 + 2 * c, 3 - 2 * c
    steps = (
        (0, 0), (0, 1), (astern, 0), (ahead, 1), (ahead, 0), (astern, 1), (2, 0), (2, 1)
    )
    fore, aft = at(dx=ahead), at(dx=astern)
    arrive = {
        1: [copies.remote(att, rows.at[1], core)],
        2: [copies.remote(att, rows.at[2], fore)],
    }
    half_rows = BLOCK // 2
    lo, hi = pl.ds(0, half_rows), pl.ds(half_rows, half_rows)

    def forward(n):
        if n == 2:
            arrive[3] = [copies.remote(rows.at[2], rows.at[3], core)]
            arrive[6] = [copies.remote(rows.at[2, lo], rows.at[6, lo], fore)]
        if n == 4:
            arrive[5] = [copies.remote(rows.at[4], rows.at[5], core)]
            arrive[6].append(copies.remote(rows.at[4, hi], rows.at[6, hi], aft))
        if n == 6:
            arrive[7] = [copies.remote(rows.at[6], rows.at[7], core)]

    quarter = BLOCK // NH
    bit = quarter // 2
    hp, hm, ho = (h + 1) % NH, (h + 3) % NH, (h + 2) % NH
    sent, sums, last = {}, {}, []
    span, feat = w_hbm.shape
    wide = NY * NZ * span

    def pair(n):
        for k in (n, n + 1):
            for copy in arrive.get(k, ()):
                copy.arrived()
            forward(k)
        got = lax.dot_general(
            rows[n:n + 2].reshape(2 * BLOCK, feat), wg[...].reshape(wide, feat), nt,
            preferred_element_type=jnp.float32,
        )
        part[n:n + 2] = got.astype(jnp.bfloat16).reshape(2, NH, quarter, wide)
        for k in (n, n + 1):
            sent[k] = (
                copies.remote(part.at[k, ho, pl.ds(0, bit)], early.at[k, 0], up),
                copies.remote(part.at[k, ho, pl.ds(bit, bit)], early.at[k, 1], down),
            )

    def plus(a, b):
        return a.astype(jnp.float32) + b.astype(jnp.float32)

    def middle(n):
        a, b = sent[n]
        a.arrived()
        area = pl.ds(0, bit)
        part[n, hp, area] = plus(part[n, hp, area], early[n, 0]).astype(jnp.bfloat16)
        there = copies.remote(part.at[n, hp], late.at[n, 0], up)
        b.arrived()
        area = pl.ds(bit, bit)
        part[n, hm, area] = plus(part[n, hm, area], early[n, 1]).astype(jnp.bfloat16)
        sums[n] = (there, copies.remote(part.at[n, hm], late.at[n, 1], down))

    def end(n):
        for copy in sums[n]:
            copy.arrived()
        done[n] = (plus(part[n, h], late[n, 0]) + late[n, 1].astype(jnp.float32)).astype(
            jnp.bfloat16
        )
        place = fin.at[x * NC + c]
        if n == 0:
            copy = pltpu.make_async_copy(done.at[0], place, local.at[4])
            copy.start()
            last.append(copy.wait)
        else:
            dx, dc = steps[n]
            last.append(copies.remote(done.at[n], place, at(dx=dx, dc=dc)).arrived)

    wa.arrived()
    wb.arrived()
    pair(0)
    middle(0)
    arrive[4] = [copies.remote(att, rows.at[4], aft)]
    middle(1)
    pair(2)
    end(0)
    middle(2)
    middle(3)
    pair(4)
    end(1)
    end(2)
    middle(4)
    middle(5)
    pair(6)
    end(3)
    end(4)
    middle(6)
    middle(7)
    end(5)
    end(6)
    end(7)
    for wait in last:
        wait()
    for n, shift in enumerate((0, 3, 1, 2)):
        for zz in range(NZ):
            cut = slice((n * NZ + zz) * span, (n * NZ + zz + 1) * span)
            size = GROUP * span
            start = (zz * NY + (y + shift) % NY) * size
            o_ref[:, pl.ds(pl.multiple_of(start, size), size)] = jnp.concatenate(
                [fin[g, :, cut] for g in range(GROUP)], axis=1
            )

    for cond in (None, is0, is1):
        chosen = [m for m in copies.made if m.cond is cond and m not in lifted + [zmove]]
        if cond is is0:
            chosen += lifted + [zmove]

        def drain(chosen=chosen):
            for moved in chosen:
                moved.copy.wait_send()

        drain() if cond is None else pl.when(cond)(drain)


def layer(band, picks, q, k, v, w):
    rows, feat = q.shape
    dt = q.dtype
    quarter = rows // NH
    wide = NY * NZ * w.shape[0]
    hbm = pl.BlockSpec(memory_space=pltpu.HBM)
    vmem = pl.BlockSpec(memory_space=pltpu.VMEM)
    smem = pl.BlockSpec(memory_space=pltpu.SMEM)
    return pl.pallas_call(
        kernel,
        out_shape=jax.ShapeDtypeStruct((quarter, GROUP * wide), dt),
        in_specs=[smem, vmem, hbm, hbm, hbm, hbm],
        out_specs=vmem,
        scratch_shapes=[
            pltpu.VMEM((3, rows, feat), dt),
            pltpu.VMEM((2, NX, NC, NY, NZ, SUMS, feat), dt),
            pltpu.VMEM((2, HALF, feat), dt),
            pltpu.VMEM((NY, NZ) + w.shape, dt),
            pltpu.VMEM((rows, feat), jnp.float32),
            pltpu.VMEM((HEADS, 1, rows), jnp.float32),
            pltpu.VMEM((HEADS, 1, rows), jnp.float32),
            pltpu.VMEM((GROUP, rows, feat), dt),
            pltpu.VMEM((GROUP, NH, quarter, wide), dt),
            pltpu.VMEM((GROUP, 2, quarter // 2, wide), dt),
            pltpu.VMEM((GROUP, 2, quarter, wide), dt),
            pltpu.VMEM((GROUP, quarter, wide), dt),
            pltpu.VMEM((GROUP, quarter, wide), dt),
            pltpu.SemaphoreType.DMA((COPIES,)),
            pltpu.SemaphoreType.DMA((COPIES,)),
            pltpu.SemaphoreType.DMA((5,)),
        ],
        compiler_params=pltpu.CompilerParams(
            collective_id=0, has_side_effects=True, vmem_limit_bytes=56 << 20
        ),
        name="layer",
    )(band, picks, q, k, v, w)


def local(queries, keys, values, band, picks, w_out):
    return layer(band, picks, queries, keys, values, w_out)


def solution(mesh):
    placed = (
        P("seq", "head"),
        P("seq", "head"),
        P("seq", "head"),
        P("head"),
        P("seq", None),
        P("seq", "head"),
    )
    return jax.shard_map(
        local, mesh=mesh, in_specs=placed, out_specs=P(("seq", "head"), None), check_vma=False
    )
```

```python
import math

import jax
import jax.numpy as jnp
from jax import lax
from jax.experimental import pallas as pl
from jax.experimental.pallas import tpu as pltpu
from jax.sharding import PartitionSpec as P

BLOCK = 128
HALF = 64
HD = 128
SUMS = 16
HEADS = 12
NX, NY, NZ, NC, NH = 4, 4, 2, 2, 4
GROUP = NX * NC
NEG = -1e30
MESH = pl.DeviceIdType.MESH
COPIES = 160


def device(z, y, x, c, h):
    return (((z * NY + y) * NX + x) * NC + c, h)


class Moved:
    def __init__(self, copy, cond):
        self.copy, self.cond = copy, cond

    def _run(self, what):
        if self.cond is None:
            what()
        else:
            pl.when(self.cond)(what)

    def start(self):
        self._run(self.copy.start)

    def arrived(self):
        self._run(self.copy.wait_recv)


class Copies:
    def __init__(self, send, recv):
        self.send, self.recv = send, recv
        self.made = []

    def remote(self, src, dst, to, cond=None, start=True):
        n = len(self.made)
        copy = pltpu.make_async_remote_copy(
            src_ref=src,
            dst_ref=dst,
            send_sem=self.send.at[n],
            recv_sem=self.recv.at[n],
            device_id=to,
            device_id_type=MESH,
        )
        moved = Moved(copy, cond)
        self.made.append(moved)
        if start:
            moved.start()
        return moved


def greet(partners):
    barrier = pltpu.get_barrier_semaphore()
    for partner in partners:
        pl.semaphore_signal(barrier, inc=1, device_id=partner, device_id_type=MESH)
    return lambda: pl.semaphore_wait(barrier, len(partners))


def kernel(
    band_ref, picks_ref, q_hbm, k_hbm, v_hbm, w_hbm, o_ref,
    qkv, kv, tails, wg, acc, top, tot, rows, part, early, late, done, fin,
    send, recv, local,
):
    s = lax.axis_index("seq")
    h = lax.axis_index("head")
    z, y, x, c = s // 32, (s // 8) % NY, (s // 2) % NX, s % 2
    at = lambda dz=0, dy=0, dx=0, dc=0, dh=0: device(
        (z + dz) % NZ, (y + dy) % NY, (x + dx) % NX, (c + dc) % NC, (h + dh) % NH
    )
    zl, core = at(dz=1), at(dc=1)
    xr, xl, yr, yl = at(dx=1), at(dx=3), at(dy=1), at(dy=3)
    up, down = at(dh=1), at(dh=3)
    after, before = ((s + 1) % 64, h), ((s + 63) % 64, h)
    is0, is1 = z == 0, z == 1
    ym, yp, yo = (y + 3) % NY, (y + 1) % NY, (y + 2) % NY
    xm, xp, xo = (x + 3) % NX, (x + 1) % NX, (x + 2) % NX
    copies = Copies(send, recv)

    loads = []
    for n, ref in enumerate((q_hbm, k_hbm, v_hbm)):
        copy = pltpu.make_async_copy(ref, qkv.at[n], local.at[n])
        copy.start()
        loads.append(copy)
    wown = pltpu.make_async_copy(w_hbm, wg.at[0, z], local.at[3])
    wown.start()
    others = [at(dx=dx, dc=dc) for dx in range(NX) for dc in range(NC) if dx or dc]
    greeted = greet([zl, yr, yl, after, before, up, down] + others)

    loads[1].wait()
    loads[2].wait()
    spot = lax.broadcasted_iota(jnp.int32, (BLOCK, SUMS), 0)
    chosen = (spot == picks_ref[...]).astype(jnp.bfloat16)
    for i in range(2):
        kv[i, x, c, y, z] = lax.dot_general(
            chosen, qkv[1 + i], (((0,), (0,)), ((), ())), preferred_element_type=jnp.float32
        ).astype(jnp.bfloat16)
    greeted()
    tail = pl.ds(BLOCK - HALF, HALF)
    behind = [
        copies.remote(qkv.at[1, tail], tails.at[0], after),
        copies.remote(qkv.at[2, tail], tails.at[1], after),
    ]
    mine = kv.at[:, x, c, y, 0]
    zmove = copies.remote(mine, mine, zl, start=False)
    pl.when(is0)(zmove.copy.start)
    zparts = ((1, is1), (0, None))
    along = {}

    def spread(row, n, zz, cond):
        keys, vals = kv.at[0, x, c, row, zz], kv.at[1, x, c, row, zz]
        both = is1 if zz else is0
        along[n, zz] = (
            copies.remote(keys, keys, xr, cond),
            copies.remote(vals, vals, xl, cond),
            copies.remote(vals, vals, xr, both),
            copies.remote(keys, keys, xl, both),
        )

    first, second = {}, {}
    for zz, cond in zparts:
        if zz == 0:
            pl.when(is1)(zmove.copy.wait_recv)
        here = kv.at[:, x, c, y, zz]
        first[zz] = (copies.remote(here, here, yr, cond), copies.remote(here, here, yl, cond))
        spread(y, 0, zz, cond)
    wown.wait()
    here = wg.at[0, z]
    wz = copies.remote(here, here, zl)

    factor = math.log2(math.e) / math.sqrt(HD)
    nt = (((1,), (1,)), ((), ()))

    def absorb(head, keys, vals, score, fresh):
        cols = pl.ds(head * HD, HD)
        most = jnp.max(score, axis=0, keepdims=True)
        if not fresh:
            old = top[head]
            most = jnp.maximum(old, most)
        weight = jnp.exp2((score - most) * factor)
        total = jnp.sum(weight, axis=0, keepdims=True)
        mixed = lax.dot_general(
            vals, weight.astype(jnp.bfloat16), (((0,), (0,)), ((), ())),
            preferred_element_type=jnp.float32,
        )
        if not fresh:
            fade = jnp.exp2((old - most) * factor)
            total = total + tot[head] * fade
            mixed = mixed + acc[:, cols] * fade
        top[head], tot[head] = most, total
        acc[:, cols] = mixed

    def near_part():
        key = lax.broadcasted_iota(jnp.int32, (BLOCK + HALF, BLOCK), 0)
        query = lax.broadcasted_iota(jnp.int32, (BLOCK + HALF, BLOCK), 1)
        back = query + HALF - key
        causal = (back >= 0) & ((key >= HALF) | (s > 0))
        for head in range(HEADS):
            cols = pl.ds(head * HD, HD)
            keys = jnp.concatenate([tails[0, :, cols], qkv[1, :, cols]], 0)
            vals = jnp.concatenate([tails[1, :, cols], qkv[2, :, cols]], 0)
            score = lax.dot_general(
                keys, qkv[0, :, cols], nt, preferred_element_type=jnp.float32
            )
            score = jnp.where(causal & (back < band_ref[head]), score, NEG)
            absorb(head, keys, vals, score, True)

    def far_part(places, planes):
        each = NC * NY * planes * SUMS
        count = each * len(places)
        shift = planes - 1
        slot = lax.broadcasted_iota(jnp.int32, (count, HD), 0)
        column = places[0]
        if len(places) == 2:
            column = jnp.where(slot < each, places[0], places[1])
        owner = (
            ((slot >> 4) & shift) * 32 + ((slot >> (4 + shift)) & 3) * 8
            + column * 2 + ((slot >> (6 + shift)) & 1)
        )
        bias = jnp.where(owner < s, 0.0, NEG)
        for head in range(HEADS):
            cols = pl.ds(head * HD, HD)
            keys, vals = (
                jnp.concatenate(
                    [kv[i, p, :, :, 0:planes, :, cols].reshape(each, HD) for p in places], 0
                )
                for i in range(2)
            )
            score = bias + lax.dot_general(
                keys, qkv[0, :, cols], nt, preferred_element_type=jnp.float32
            )
            absorb(head, keys, vals, score, False)

    for zz, cond in zparts:
        first[zz][0].arrived()
        piece = kv.at[0, x, c, ym, zz]
        a = copies.remote(piece, piece, yr, cond)
        spread(ym, 1, zz, cond)
        first[zz][1].arrived()
        piece = kv.at[1, x, c, yp, zz]
        b = copies.remote(piece, piece, yl, cond)
        spread(yp, 2, zz, cond)
        second[zz] = (a, b)

    def both_ways(zz):
        here = wg.at[0, zz]
        return (copies.remote(here, wg.at[1, zz], yr), copies.remote(here, wg.at[2, zz], yl))

    wfirst = both_ways(z)
    for zz, cond in zparts:
        for copy in second[zz]:
            copy.arrived()
        spread(yo, 3, zz, cond)
    wz.arrived()
    wlast = both_ways(1 - z)
    wa = copies.remote(wg.at[1, z], wg.at[3, z], yr, start=False)
    wb = copies.remote(wg.at[2, 1 - z], wg.at[3, 1 - z], yl, start=False)

    def w_early():
        wfirst[0].copy.wait_recv()
        wa.copy.start()

    def w_late():
        wfirst[1].copy.wait_recv()
        wlast[0].copy.wait_recv()
        wlast[1].copy.wait_recv()
        wb.copy.start()

    def across(column):
        moved = []
        for zz, cond in zparts:
            here = kv.at[:, column, c, :, zz]
            moved.append(copies.remote(here, here, core, cond))
        return moved

    opposite, lifted = [], []
    order = (y, ym, yp, yo)

    def pass_on(n):
        for zz, cond in zparts:
            both = is1 if zz else is0
            for copy in along[n, zz]:
                copy.arrived()
            row = order[n]
            keys, vals = kv.at[0, xm, c, row, zz], kv.at[1, xp, c, row, zz]
            opposite.append(copies.remote(vals, vals, xl, cond))
            if n < 2:
                opposite.append(copies.remote(keys, keys, xr, cond))
            else:
                other = kv.at[0, xp, c, row, zz]
                opposite.append(copies.remote(other, other, xl, both))
                if zz == 0:
                    opposite.append(copies.remote(keys, keys, xr, is1))
            if zz == 0:
                for there in (kv.at[1, xm, c, row, 0], kv.at[0, xp, c, row, 0]):
                    moved = copies.remote(there, there, zl, start=False)
                    pl.when(is0)(moved.copy.start)
                    lifted.append(moved)

    given = across(x)
    pass_on(0)
    loads[0].wait()
    for copy in behind:
        copy.arrived()
    near_part()
    pass_on(1)
    for copy in given:
        copy.arrived()
    pl.when(is1)(lambda: far_part([x], 2))
    pass_on(2)

    pl.when(is1)(w_early)
    pass_on(3)

    @pl.when(is1)
    def _():
        for moved in lifted:
            moved.copy.wait_recv()

    given_m, given_p = across(xm), across(xp)
    for copy in given_m:
        copy.arrived()

    @pl.when(is0)
    def _():
        far_part([x, xm], 1)
        w_early()

    @pl.when(is1)
    def _():
        far_part([xm], 2)
        w_late()

    for copy in given_p:
        copy.arrived()
    pl.when(is1)(lambda: far_part([xp], 2))
    for copy in opposite:
        copy.arrived()
    given = across(xo)
    pl.when(is0)(w_late)
    for copy in given:
        copy.arrived()
    pl.when(is0)(lambda: far_part([xp, xo], 1))
    pl.when(is1)(lambda: far_part([xo], 2))
    att = rows.at[0]
    for head in range(HEADS):
        cols = pl.ds(head * HD, HD)
        att[:, cols] = (acc[:, cols] / tot[head]).T.astype(jnp.bfloat16)

    ahead, astern = 1 + 2 * c, 3 - 2 * c
    steps = (
        (0, 0), (0, 1), (astern, 0), (ahead, 1), (ahead, 0), (astern, 1), (2, 0), (2, 1)
    )
    fore, aft = at(dx=ahead), at(dx=astern)
    arrive = {
        1: [copies.remote(att, rows.at[1], core)],
        2: [copies.remote(att, rows.at[2], fore)],
    }
    half_rows = BLOCK // 2
    lo, hi = pl.ds(0, half_rows), pl.ds(half_rows, half_rows)

    def forward(n):
        if n == 2:
            arrive[3] = [copies.remote(rows.at[2], rows.at[3], core)]
            arrive[6] = [copies.remote(rows.at[2, lo], rows.at[6, lo], fore)]
        if n == 4:
            arrive[5] = [copies.remote(rows.at[4], rows.at[5], core)]
            arrive[6].append(copies.remote(rows.at[4, hi], rows.at[6, hi], aft))
        if n == 6:
            arrive[7] = [copies.remote(rows.at[6], rows.at[7], core)]

    quarter = BLOCK // NH
    bit = quarter // 2
    hp, hm, ho = (h + 1) % NH, (h + 3) % NH, (h + 2) % NH
    sent, sums, last = {}, {}, []
    span, feat = w_hbm.shape
    wide = NY * NZ * span

    def fetch(*blocks):
        for k in blocks:
            for copy in arrive[k]:
                copy.arrived()
            forward(k)

    def pair(n):
        got = lax.dot_general(
            rows[n:n + 2].reshape(2 * BLOCK, feat), wg[...].reshape(wide, feat), nt,
            preferred_element_type=jnp.float32,
        )
        part[n:n + 2] = got.astype(jnp.bfloat16).reshape(2, NH, quarter, wide)
        for k in (n, n + 1):
            sent[k] = (
                copies.remote(part.at[k, ho, pl.ds(0, bit)], early.at[k, 0], up),
                copies.remote(part.at[k, ho, pl.ds(bit, bit)], early.at[k, 1], down),
            )

    def plus(a, b):
        return a.astype(jnp.float32) + b.astype(jnp.float32)

    def middle(n):
        a, b = sent[n]
        a.arrived()
        area = pl.ds(0, bit)
        part[n, hp, area] = plus(part[n, hp, area], early[n, 0]).astype(jnp.bfloat16)
        there = copies.remote(part.at[n, hp], late.at[n, 0], up)
        b.arrived()
        area = pl.ds(bit, bit)
        part[n, hm, area] = plus(part[n, hm, area], early[n, 1]).astype(jnp.bfloat16)
        sums[n] = (there, copies.remote(part.at[n, hm], late.at[n, 1], down))

    def end(n):
        for copy in sums[n]:
            copy.arrived()
        done[n] = (plus(part[n, h], late[n, 0]) + late[n, 1].astype(jnp.float32)).astype(
            jnp.bfloat16
        )
        place = fin.at[x * NC + c]
        if n == 0:
            copy = pltpu.make_async_copy(done.at[0], place, local.at[4])
            copy.start()
            last.append(copy.wait)
        else:
            dx, dc = steps[n]
            last.append(copies.remote(done.at[n], place, at(dx=dx, dc=dc)).arrived)

    wa.arrived()
    wb.arrived()
    fetch(1)
    pair(0)
    arrive[4] = [copies.remote(att, rows.at[4], aft)]
    middle(0)
    middle(1)
    fetch(2, 3)
    pair(2)
    middle(2)
    fetch(4)
    middle(3)
    fetch(5)
    pair(4)
    end(0)
    end(1)
    fetch(6)
    middle(4)
    middle(5)
    fetch(7)
    pair(6)
    end(2)
    end(3)
    middle(6)
    middle(7)
    end(4)
    end(5)
    end(6)
    end(7)
    for wait in last:
        wait()
    for n, shift in enumerate((0, 3, 1, 2)):
        for zz in range(NZ):
            cut = slice((n * NZ + zz) * span, (n * NZ + zz + 1) * span)
            size = GROUP * span
            start = (zz * NY + (y + shift) % NY) * size
            o_ref[:, pl.ds(pl.multiple_of(start, size), size)] = jnp.concatenate(
                [fin[g, :, cut] for g in range(GROUP)], axis=1
            )

    for cond in (None, is0, is1):
        chosen = [m for m in copies.made if m.cond is cond and m not in lifted + [zmove]]
        if cond is is0:
            chosen += lifted + [zmove]

        def drain(chosen=chosen):
            for moved in chosen:
                moved.copy.wait_send()

        drain() if cond is None else pl.when(cond)(drain)


def layer(band, picks, q, k, v, w):
    rows, feat = q.shape
    dt = q.dtype
    quarter = rows // NH
    wide = NY * NZ * w.shape[0]
    hbm = pl.BlockSpec(memory_space=pltpu.HBM)
    vmem = pl.BlockSpec(memory_space=pltpu.VMEM)
    smem = pl.BlockSpec(memory_space=pltpu.SMEM)
    return pl.pallas_call(
        kernel,
        out_shape=jax.ShapeDtypeStruct((quarter, GROUP * wide), dt),
        in_specs=[smem, vmem, hbm, hbm, hbm, hbm],
        out_specs=vmem,
        scratch_shapes=[
            pltpu.VMEM((3, rows, feat), dt),
            pltpu.VMEM((2, NX, NC, NY, NZ, SUMS, feat), dt),
            pltpu.VMEM((2, HALF, feat), dt),
            pltpu.VMEM((NY, NZ) + w.shape, dt),
            pltpu.VMEM((rows, feat), jnp.float32),
            pltpu.VMEM((HEADS, 1, rows), jnp.float32),
            pltpu.VMEM((HEADS, 1, rows), jnp.float32),
            pltpu.VMEM((GROUP, rows, feat), dt),
            pltpu.VMEM((GROUP, NH, quarter, wide), dt),
            pltpu.VMEM((GROUP, 2, quarter // 2, wide), dt),
            pltpu.VMEM((GROUP, 2, quarter, wide), dt),
            pltpu.VMEM((GROUP, quarter, wide), dt),
            pltpu.VMEM((GROUP, quarter, wide), dt),
            pltpu.SemaphoreType.DMA((COPIES,)),
            pltpu.SemaphoreType.DMA((COPIES,)),
            pltpu.SemaphoreType.DMA((5,)),
        ],
        compiler_params=pltpu.CompilerParams(
            collective_id=0, has_side_effects=True, vmem_limit_bytes=56 << 20
        ),
        name="layer",
    )(band, picks, q, k, v, w)


def local(queries, keys, values, band, picks, w_out):
    return layer(band, picks, queries, keys, values, w_out)


def solution(mesh):
    placed = (
        P("seq", "head"),
        P("seq", "head"),
        P("seq", "head"),
        P("head"),
        P("seq", None),
        P("seq", "head"),
    )
    return jax.shard_map(
        local, mesh=mesh, in_specs=placed, out_specs=P(("seq", "head"), None), check_vma=False
    )
```

```python
import math

import jax
import jax.numpy as jnp
from jax import lax
from jax.experimental import pallas as pl
from jax.experimental.pallas import tpu as pltpu
from jax.sharding import PartitionSpec as P

BLOCK = 128
HALF = 64
HD = 128
SUMS = 16
HEADS = 12
NX, NY, NZ, NC, NH = 4, 4, 2, 2, 4
GROUP = NX * NC
NEG = -1e30
MESH = pl.DeviceIdType.MESH
COPIES = 160


def device(z, y, x, c, h):
    return (((z * NY + y) * NX + x) * NC + c, h)


class Moved:
    def __init__(self, copy, cond):
        self.copy, self.cond = copy, cond

    def _run(self, what):
        if self.cond is None:
            what()
        else:
            pl.when(self.cond)(what)

    def start(self):
        self._run(self.copy.start)

    def arrived(self):
        self._run(self.copy.wait_recv)


class Copies:
    def __init__(self, send, recv):
        self.send, self.recv = send, recv
        self.made = []

    def remote(self, src, dst, to, cond=None, start=True):
        n = len(self.made)
        copy = pltpu.make_async_remote_copy(
            src_ref=src,
            dst_ref=dst,
            send_sem=self.send.at[n],
            recv_sem=self.recv.at[n],
            device_id=to,
            device_id_type=MESH,
        )
        moved = Moved(copy, cond)
        self.made.append(moved)
        if start:
            moved.start()
        return moved


def greet(partners):
    barrier = pltpu.get_barrier_semaphore()
    for partner in partners:
        pl.semaphore_signal(barrier, inc=1, device_id=partner, device_id_type=MESH)
    return lambda: pl.semaphore_wait(barrier, len(partners))


def kernel(
    band_ref, picks_ref, q_hbm, k_hbm, v_hbm, w_hbm, o_ref,
    qkv, kv, tails, wg, acc, top, tot, rows, part, early, late, done, fin,
    send, recv, local,
):
    s = lax.axis_index("seq")
    h = lax.axis_index("head")
    z, y, x, c = s // 32, (s // 8) % NY, (s // 2) % NX, s % 2
    at = lambda dz=0, dy=0, dx=0, dc=0, dh=0: device(
        (z + dz) % NZ, (y + dy) % NY, (x + dx) % NX, (c + dc) % NC, (h + dh) % NH
    )
    zl, core = at(dz=1), at(dc=1)
    xr, xl, yr, yl = at(dx=1), at(dx=3), at(dy=1), at(dy=3)
    up, down = at(dh=1), at(dh=3)
    after, before = ((s + 1) % 64, h), ((s + 63) % 64, h)
    is0, is1 = z == 0, z == 1
    ym, yp, yo = (y + 3) % NY, (y + 1) % NY, (y + 2) % NY
    xm, xp, xo = (x + 3) % NX, (x + 1) % NX, (x + 2) % NX
    copies = Copies(send, recv)

    loads = []
    for n, ref in enumerate((q_hbm, k_hbm, v_hbm)):
        copy = pltpu.make_async_copy(ref, qkv.at[n], local.at[n])
        copy.start()
        loads.append(copy)
    wown = pltpu.make_async_copy(w_hbm, wg.at[0, z], local.at[3])
    wown.start()
    others = [at(dx=dx, dc=dc) for dx in range(NX) for dc in range(NC) if dx or dc]
    greeted = greet([zl, yr, yl, after, before, up, down] + others)

    loads[1].wait()
    loads[2].wait()
    spot = lax.broadcasted_iota(jnp.int32, (BLOCK, SUMS), 0)
    chosen = (spot == picks_ref[...]).astype(jnp.bfloat16)
    for i in range(2):
        kv[i, x, c, y, z] = lax.dot_general(
            chosen, qkv[1 + i], (((0,), (0,)), ((), ())), preferred_element_type=jnp.float32
        ).astype(jnp.bfloat16)
    greeted()
    tail = pl.ds(BLOCK - HALF, HALF)
    behind = [
        copies.remote(qkv.at[1, tail], tails.at[0], after),
        copies.remote(qkv.at[2, tail], tails.at[1], after),
    ]
    mine = kv.at[:, x, c, y, 0]
    zmove = copies.remote(mine, mine, zl, start=False)
    pl.when(is0)(zmove.copy.start)
    zparts = ((1, is1), (0, None))
    along = {}

    def spread(row, n, zz, cond):
        keys, vals = kv.at[0, x, c, row, zz], kv.at[1, x, c, row, zz]
        both = is1 if zz else is0
        along[n, zz] = (
            copies.remote(keys, keys, xr, cond),
            copies.remote(vals, vals, xl, cond),
            copies.remote(vals, vals, xr, both),
            copies.remote(keys, keys, xl, both),
        )

    first, second = {}, {}
    for zz, cond in zparts:
        if zz == 0:
            pl.when(is1)(zmove.copy.wait_recv)
        here = kv.at[:, x, c, y, zz]
        first[zz] = (copies.remote(here, here, yr, cond), copies.remote(here, here, yl, cond))
        spread(y, 0, zz, cond)
    wown.wait()
    here = wg.at[0, z]
    wz = copies.remote(here, here, zl)

    factor = math.log2(math.e) / math.sqrt(HD)
    nt = (((1,), (1,)), ((), ()))

    def absorb(head, keys, vals, score, fresh):
        cols = pl.ds(head * HD, HD)
        most = jnp.max(score, axis=0, keepdims=True)
        if not fresh:
            old = top[head]
            most = jnp.maximum(old, most)
        weight = jnp.exp2((score - most) * factor)
        total = jnp.sum(weight, axis=0, keepdims=True)
        mixed = lax.dot_general(
            vals, weight.astype(jnp.bfloat16), (((0,), (0,)), ((), ())),
            preferred_element_type=jnp.float32,
        )
        if not fresh:
            fade = jnp.exp2((old - most) * factor)
            total = total + tot[head] * fade
            mixed = mixed + acc[:, cols] * fade
        top[head], tot[head] = most, total
        acc[:, cols] = mixed

    def near_part():
        key = lax.broadcasted_iota(jnp.int32, (BLOCK + HALF, BLOCK), 0)
        query = lax.broadcasted_iota(jnp.int32, (BLOCK + HALF, BLOCK), 1)
        back = query + HALF - key
        causal = (back >= 0) & ((key >= HALF) | (s > 0))
        for head in range(HEADS):
            cols = pl.ds(head * HD, HD)
            keys = jnp.concatenate([tails[0, :, cols], qkv[1, :, cols]], 0)
            vals = jnp.concatenate([tails[1, :, cols], qkv[2, :, cols]], 0)
            score = lax.dot_general(
                keys, qkv[0, :, cols], nt, preferred_element_type=jnp.float32
            )
            score = jnp.where(causal & (back < band_ref[head]), score, NEG)
            absorb(head, keys, vals, score, True)

    def far_part(places, planes):
        each = NC * NY * planes * SUMS
        count = each * len(places)
        shift = planes - 1
        slot = lax.broadcasted_iota(jnp.int32, (count, HD), 0)
        column = places[0]
        if len(places) == 2:
            column = jnp.where(slot < each, places[0], places[1])
        owner = (
            ((slot >> 4) & shift) * 32 + ((slot >> (4 + shift)) & 3) * 8
            + column * 2 + ((slot >> (6 + shift)) & 1)
        )
        bias = jnp.where(owner < s, 0.0, NEG)
        for head in range(HEADS):
            cols = pl.ds(head * HD, HD)
            keys, vals = (
                jnp.concatenate(
                    [kv[i, p, :, :, 0:planes, :, cols].reshape(each, HD) for p in places], 0
                )
                for i in range(2)
            )
            score = bias + lax.dot_general(
                keys, qkv[0, :, cols], nt, preferred_element_type=jnp.float32
            )
            absorb(head, keys, vals, score, False)

    for zz, cond in zparts:
        first[zz][0].arrived()
        piece = kv.at[0, x, c, ym, zz]
        a = copies.remote(piece, piece, yr, cond)
        spread(ym, 1, zz, cond)
        first[zz][1].arrived()
        piece = kv.at[1, x, c, yp, zz]
        b = copies.remote(piece, piece, yl, cond)
        spread(yp, 2, zz, cond)
        second[zz] = (a, b)

    def both_ways(zz):
        here = wg.at[0, zz]
        return (copies.remote(here, wg.at[1, zz], yr), copies.remote(here, wg.at[2, zz], yl))

    wfirst = both_ways(z)
    for zz, cond in zparts:
        for copy in second[zz]:
            copy.arrived()
        spread(yo, 3, zz, cond)
    wz.arrived()
    wlast = both_ways(1 - z)
    wa = copies.remote(wg.at[1, z], wg.at[3, z], yr, start=False)
    wb = copies.remote(wg.at[2, 1 - z], wg.at[3, 1 - z], yl, start=False)

    def w_early():
        wfirst[0].copy.wait_recv()
        wa.copy.start()

    def w_late():
        wfirst[1].copy.wait_recv()
        wlast[0].copy.wait_recv()
        wlast[1].copy.wait_recv()
        wb.copy.start()

    def across(column):
        moved = []
        for zz, cond in zparts:
            here = kv.at[:, column, c, :, zz]
            moved.append(copies.remote(here, here, core, cond))
        return moved

    opposite, lifted = [], []
    order = (y, ym, yp, yo)

    def pass_on(n):
        for zz, cond in zparts:
            both = is1 if zz else is0
            for copy in along[n, zz]:
                copy.arrived()
            row = order[n]
            keys, vals = kv.at[0, xm, c, row, zz], kv.at[1, xp, c, row, zz]
            opposite.append(copies.remote(vals, vals, xl, cond))
            if n < 2:
                opposite.append(copies.remote(keys, keys, xr, cond))
            else:
                other = kv.at[0, xp, c, row, zz]
                opposite.append(copies.remote(other, other, xl, both))
                if zz == 0:
                    opposite.append(copies.remote(keys, keys, xr, is1))
            if zz == 0:
                for there in (kv.at[1, xm, c, row, 0], kv.at[0, xp, c, row, 0]):
                    moved = copies.remote(there, there, zl, start=False)
                    pl.when(is0)(moved.copy.start)
                    lifted.append(moved)

    given = across(x)
    pass_on(0)
    loads[0].wait()
    for copy in behind:
        copy.arrived()
    near_part()
    pass_on(1)
    for copy in given:
        copy.arrived()
    pl.when(is1)(lambda: far_part([x], 2))
    pass_on(2)

    pl.when(is1)(w_early)
    pass_on(3)

    @pl.when(is1)
    def _():
        for moved in lifted:
            moved.copy.wait_recv()

    given_m, given_p = across(xm), across(xp)
    for copy in given_m:
        copy.arrived()

    @pl.when(is0)
    def _():
        far_part([x, xm], 1)
        w_early()

    @pl.when(is1)
    def _():
        far_part([xm], 2)
        w_late()

    for copy in given_p:
        copy.arrived()
    pl.when(is1)(lambda: far_part([xp], 2))
    for copy in opposite:
        copy.arrived()
    given = across(xo)
    pl.when(is0)(w_late)
    for copy in given:
        copy.arrived()
    pl.when(is0)(lambda: far_part([xp, xo], 1))
    pl.when(is1)(lambda: far_part([xo], 2))
    att = rows.at[0]
    for head in range(HEADS):
        cols = pl.ds(head * HD, HD)
        att[:, cols] = (acc[:, cols] / tot[head]).T.astype(jnp.bfloat16)

    ahead, astern = 1 + 2 * c, 3 - 2 * c
    steps = (
        (0, 0), (0, 1), (astern, 0), (ahead, 1), (ahead, 0), (astern, 1), (2, 0), (2, 1)
    )
    fore, aft = at(dx=ahead), at(dx=astern)
    arrive = {
        1: [copies.remote(att, rows.at[1], core)],
        2: [copies.remote(att, rows.at[2], fore)],
    }
    half_rows = BLOCK // 2
    lo, hi = pl.ds(0, half_rows), pl.ds(half_rows, half_rows)

    def forward(n):
        if n == 2:
            arrive[3] = [copies.remote(rows.at[2], rows.at[3], core)]
            arrive[6] = [copies.remote(rows.at[2, lo], rows.at[6, lo], fore)]
        if n == 4:
            arrive[5] = [copies.remote(rows.at[4], rows.at[5], core)]
            arrive[6].append(copies.remote(rows.at[4, hi], rows.at[6, hi], aft))
        if n == 6:
            arrive[7] = [copies.remote(rows.at[6], rows.at[7], core)]

    quarter = BLOCK // NH
    bit = quarter // 2
    hp, hm, ho = (h + 1) % NH, (h + 3) % NH, (h + 2) % NH
    sent, sums, last = {}, {}, []
    span, feat = w_hbm.shape
    wide = NY * NZ * span

    def fetch(*blocks):
        for k in blocks:
            for copy in arrive[k]:
                copy.arrived()
            forward(k)

    def pair(n):
        got = lax.dot_general(
            rows[n:n + 2].reshape(2 * BLOCK, feat), wg[...].reshape(wide, feat), nt,
            preferred_element_type=jnp.float32,
        )
        part[n:n + 2] = got.astype(jnp.bfloat16).reshape(2, NH, quarter, wide)
        for k in (n, n + 1):
            sent[k] = (
                copies.remote(part.at[k, ho, pl.ds(0, bit)], early.at[k, 0], up),
                copies.remote(part.at[k, ho, pl.ds(bit, bit)], early.at[k, 1], down),
            )

    def plus(a, b):
        return a.astype(jnp.float32) + b.astype(jnp.float32)

    def middle(n):
        a, b = sent[n]
        a.arrived()
        area = pl.ds(0, bit)
        part[n, hp, area] = plus(part[n, hp, area], early[n, 0]).astype(jnp.bfloat16)
        there = copies.remote(part.at[n, hp], late.at[n, 0], up)
        b.arrived()
        area = pl.ds(bit, bit)
        part[n, hm, area] = plus(part[n, hm, area], early[n, 1]).astype(jnp.bfloat16)
        sums[n] = (there, copies.remote(part.at[n, hm], late.at[n, 1], down))

    def end(n):
        for copy in sums[n]:
            copy.arrived()
        done[n] = (plus(part[n, h], late[n, 0]) + late[n, 1].astype(jnp.float32)).astype(
            jnp.bfloat16
        )
        place = fin.at[x * NC + c]
        if n == 0:
            copy = pltpu.make_async_copy(done.at[0], place, local.at[4])
            copy.start()
            last.append(copy.wait)
        else:
            dx, dc = steps[n]
            last.append(copies.remote(done.at[n], place, at(dx=dx, dc=dc)).arrived)

    wa.arrived()
    wb.arrived()
    arrive[4] = [copies.remote(att, rows.at[4], aft)]
    fetch(1)
    pair(0)
    middle(0)
    middle(1)
    fetch(2, 3)
    pair(2)
    fetch(4)
    end(0)
    middle(2)
    middle(3)
    fetch(5)
    pair(4)
    fetch(6)
    end(1)
    end(2)
    middle(4)
    middle(5)
    fetch(7)
    pair(6)
    end(3)
    end(4)
    middle(6)
    middle(7)
    end(5)
    end(6)
    end(7)
    for wait in last:
        wait()
    for n, shift in enumerate((0, 3, 1, 2)):
        for zz in range(NZ):
            cut = slice((n * NZ + zz) * span, (n * NZ + zz + 1) * span)
            size = GROUP * span
            start = (zz * NY + (y + shift) % NY) * size
            o_ref[:, pl.ds(pl.multiple_of(start, size), size)] = jnp.concatenate(
                [fin[g, :, cut] for g in range(GROUP)], axis=1
            )

    for cond in (None, is0, is1):
        chosen = [m for m in copies.made if m.cond is cond and m not in lifted + [zmove]]
        if cond is is0:
            chosen += lifted + [zmove]

        def drain(chosen=chosen):
            for moved in chosen:
                moved.copy.wait_send()

        drain() if cond is None else pl.when(cond)(drain)


def layer(band, picks, q, k, v, w):
    rows, feat = q.shape
    dt = q.dtype
    quarter = rows // NH
    wide = NY * NZ * w.shape[0]
    hbm = pl.BlockSpec(memory_space=pltpu.HBM)
    vmem = pl.BlockSpec(memory_space=pltpu.VMEM)
    smem = pl.BlockSpec(memory_space=pltpu.SMEM)
    return pl.pallas_call(
        kernel,
        out_shape=jax.ShapeDtypeStruct((quarter, GROUP * wide), dt),
        in_specs=[smem, vmem, hbm, hbm, hbm, hbm],
        out_specs=vmem,
        scratch_shapes=[
            pltpu.VMEM((3, rows, feat), dt),
            pltpu.VMEM((2, NX, NC, NY, NZ, SUMS, feat), dt),
            pltpu.VMEM((2, HALF, feat), dt),
            pltpu.VMEM((NY, NZ) + w.shape, dt),
            pltpu.VMEM((rows, feat), jnp.float32),
            pltpu.VMEM((HEADS, 1, rows), jnp.float32),
            pltpu.VMEM((HEADS, 1, rows), jnp.float32),
            pltpu.VMEM((GROUP, rows, feat), dt),
            pltpu.VMEM((GROUP, NH, quarter, wide), dt),
            pltpu.VMEM((GROUP, 2, quarter // 2, wide), dt),
            pltpu.VMEM((GROUP, 2, quarter, wide), dt),
            pltpu.VMEM((GROUP, quarter, wide), dt),
            pltpu.VMEM((GROUP, quarter, wide), dt),
            pltpu.SemaphoreType.DMA((COPIES,)),
            pltpu.SemaphoreType.DMA((COPIES,)),
            pltpu.SemaphoreType.DMA((5,)),
        ],
        compiler_params=pltpu.CompilerParams(
            collective_id=0, has_side_effects=True, vmem_limit_bytes=56 << 20
        ),
        name="layer",
    )(band, picks, q, k, v, w)


def local(queries, keys, values, band, picks, w_out):
    return layer(band, picks, queries, keys, values, w_out)


def solution(mesh):
    placed = (
        P("seq", "head"),
        P("seq", "head"),
        P("seq", "head"),
        P("head"),
        P("seq", None),
        P("seq", "head"),
    )
    return jax.shard_map(
        local, mesh=mesh, in_specs=placed, out_specs=P(("seq", "head"), None), check_vma=False
    )
```
